128 devices in a mesh: strip: 32 (over z_hi, x, y), dict: 4 (over z_lo, core).
Axes of the slice: x: 4, y: 4, z: 4 (z_hi: 2, z_lo: 2; z = z_hi * 2 + z_lo), core: 2. Of those that a mesh axis runs over, the one named last changes fastest.
Arguments:
- patterns: bfloat16 [3600, 256, 512], P(None, 'strip', 'dict'), may hold values from -100 to 160
- scan_mask: int32 [256, 512], P('strip', 'dict'), may hold values 0 or 1
- neighbour_mask: int32 [8, 256, 512], P(None, 'strip', 'dict'), may hold values 0 or 1
- dictionary: bfloat16 [2, 512, 3600], P(None, ('strip', 'dict')), may hold values from -160 to 160
Outputs:
- top_scores: float32 [2, 4, 256, 512], P(None, None, 'strip', 'dict')
The draws below stay inside these ranges and needn't reach their ends.
All inputs are finite; a program needn't handle non-finite values. No bound on the sum of `scan_mask` or of `neighbour_mask` on one device may be relied on, other than what follows from the above.
Results may differ from the reference program's by a relative error of at most 0.00081.
Values may be sent and summed in bfloat16 or wider, within the bound.
A program may use at most 192 MiB of HBM per device.

```python
import math
import jax
import jax.numpy as jnp
from jax import lax

PH = 60
PANELS = 2
ENTRIES = 512
TOP = 4
ROWS_DEV = 8
ROWS = 256
COLS = 512


def dictionary_core(key):
    k_base, k_entry, k_pixel = jax.random.split(jax.random.fold_in(key, 11), 3)
    base_values = jnp.clip(jax.random.normal(k_base, (PANELS * ENTRIES, PH * PH), jnp.float32), -4.0, 4.0)
    pixel_scale = jnp.exp(jax.random.uniform(k_pixel, (1, PH * PH), jnp.float32, 0.0, math.log(4.0)))
    entry_scale = jnp.exp(jax.random.uniform(k_entry, (PANELS * ENTRIES, 1), jnp.float32, 0.0, math.log(10.0)))
    return (base_values * pixel_scale, entry_scale)


def draw_dictionary(key, part):
    unit_rows, entry_scale = dictionary_core(key)
    return (unit_rows * entry_scale).reshape(PANELS, ENTRIES, PH * PH).astype(jnp.bfloat16)


def draw_patterns(key, part):
    unit_rows, entry_scale = dictionary_core(key)
    k_id, k_noise, k_amp, k_back, k_row, k_col = jax.random.split(jax.random.fold_in(key, 23), 6)
    orient_ids = jax.random.randint(k_id, (ROWS, COLS), 0, PANELS * ENTRIES)
    signal_part = jnp.take(unit_rows.T, orient_ids, axis=1) * 0.5
    noise_part = 0.5 * jnp.clip(jax.random.normal(k_noise, (PH * PH, ROWS, COLS), jnp.float32), -4.0, 4.0)
    back_level = jax.random.uniform(k_back, (ROWS, COLS), jnp.float32, 2.0, 6.0)
    amplitude = jnp.exp(jax.random.uniform(k_amp, (ROWS, COLS), jnp.float32, 0.0, math.log(10.0)))
    centre_row = jax.random.uniform(k_row, (ROWS, COLS), jnp.float32, 0.3 * PH, 0.7 * PH)
    centre_col = jax.random.uniform(k_col, (ROWS, COLS), jnp.float32, 0.3 * PH, 0.7 * PH)
    pixel_ids = jnp.arange(PH * PH, dtype=jnp.int32)
    detector_row = (pixel_ids // PH).astype(jnp.float32)[:, None, None]
    detector_col = (pixel_ids % PH).astype(jnp.float32)[:, None, None]
    bump_width = 0.4 * PH
    bump_shape = jnp.exp(-((detector_row - centre_row) ** 2 + (detector_col - centre_col) ** 2) / (2.0 * bump_width * bump_width))
    return (amplitude * (signal_part + noise_part) + back_level * amplitude * bump_shape).astype(jnp.bfloat16)


def touch_ends(result, own_key, smallest, top_value):
    dims = result.shape
    index_at = [jax.random.randint(jax.random.fold_in(own_key, axis), (), 0, dims[axis]) for axis in range(len(dims))]
    result = result.at[tuple(index_at)].set(smallest)
    longest = dims.index(max(dims))
    index_at[longest] = (index_at[longest] + 1) % dims[longest]
    return result.at[tuple(index_at)].set(top_value)


def setup_inputs(seed: int = 0) -> dict:
    splits = jax.random.split(jax.random.key(seed), 5)
    return {
        "patterns": draw_patterns(jax.random.fold_in(splits[4], 71), 0),
        "scan_mask": touch_ends((jax.random.randint(splits[1], (ROWS, COLS), 0, 8) < 7).astype(jnp.int32), jax.random.fold_in(splits[1], 1), 0, 1),
        "neighbour_mask": touch_ends((jax.random.randint(splits[2], (8, ROWS, COLS), 0, 2) < 1).astype(jnp.int32), jax.random.fold_in(splits[2], 1), 0, 1),
        "dictionary": draw_dictionary(jax.random.fold_in(splits[4], 71), 0),
    }


epsilon = 1e-05
nlpar_scale = 2.0

def blur_matrix():
    positions = jnp.arange(PH, dtype=jnp.int32).astype(jnp.float32)
    spread_px = PH / 8.0
    profile = jnp.exp(-(positions[:, None] - positions[None, :]) ** 2 / (2.0 * spread_px * spread_px))
    return (profile / lax.optimization_barrier(jnp.sum(profile, axis=1, keepdims=True))).astype(jnp.bfloat16)

def standardize(row_block, kernel):
    block_shape = row_block.shape
    detector = row_block.reshape(PH, PH, -1).astype(jnp.float32)
    kernel32 = kernel.astype(jnp.float32)
    half_pass = jnp.einsum('abm,db->adm', detector, kernel32).astype(jnp.bfloat16)
    background = jnp.einsum('abm,ea->ebm', half_pass.astype(jnp.float32), kernel32)
    corrected = detector - background
    centre_mean = lax.optimization_barrier(jnp.mean(corrected, axis=(0, 1), keepdims=True))
    centred = corrected - centre_mean
    variance = lax.optimization_barrier(jnp.mean(centred * centred, axis=(0, 1), keepdims=True))
    return (centred / jnp.sqrt(variance + epsilon)).astype(jnp.bfloat16).reshape(block_shape)

def neighbour_average(padded, mask_rows, first_row, first_col, all_rows, all_cols):
    row_count = padded.shape[1] - 2
    col_count = padded.shape[2] - 2
    centre = padded[:, 1:row_count + 1, 1:col_count + 1].astype(jnp.float32)
    row_at = first_row + jnp.arange(row_count, dtype=jnp.int32)
    col_at = first_col + jnp.arange(col_count, dtype=jnp.int32)
    numerator = centre
    weight_sum = jnp.ones((row_count, col_count), jnp.float32)
    slot_index = 0
    for row_step in (-1, 0, 1):
        for col_step in (-1, 0, 1):
            if row_step == 0 and col_step == 0:
                continue
            beside = padded[:, 1 + row_step:1 + row_step + row_count, 1 + col_step:1 + col_step + col_count].astype(jnp.float32)
            differ = centre - beside
            distance = lax.optimization_barrier(jnp.mean(differ * differ, axis=0))
            row_ok = (row_at + row_step >= 0) & (row_at + row_step < all_rows)
            col_ok = (col_at + col_step >= 0) & (col_at + col_step < all_cols)
            usable = row_ok[:, None] & col_ok[None, :] & (mask_rows[slot_index] == 1)
            weight = jnp.where(usable, jnp.exp(-distance / nlpar_scale), jnp.zeros_like(distance))
            numerator = numerator + weight[None] * beside
            weight_sum = weight_sum + weight
            slot_index += 1
    return (numerator / weight_sum[None]).astype(jnp.bfloat16)

def reference(patterns, scan_mask, neighbour_mask, dictionary):
    kernel = blur_matrix()
    masked = patterns * scan_mask.astype(jnp.bfloat16)[None]
    block_count = ROWS // ROWS_DEV
    pixel_count = PH * PH

    def standard_block(index):
        row_block = lax.dynamic_slice_in_dim(masked, index * ROWS_DEV, ROWS_DEV, axis=1)
        return standardize(row_block, kernel)
    stacked = lax.map(standard_block, jnp.arange(block_count, dtype=jnp.int32))
    standard = jnp.moveaxis(stacked, 0, 1).reshape(pixel_count, ROWS, COLS)
    padded = jnp.pad(standard, ((0, 0), (1, 1), (1, 1)))
    dictionary32 = dictionary.astype(jnp.float32)
    inv_entry = 1.0 / jnp.sqrt(lax.optimization_barrier(jnp.mean(dictionary32 * dictionary32, axis=2)) + epsilon)

    def score_rows(index):
        first_row = index * ROWS_DEV
        window = lax.dynamic_slice_in_dim(padded, first_row, ROWS_DEV + 2, axis=1)
        mask_rows = lax.dynamic_slice_in_dim(neighbour_mask, first_row, ROWS_DEV, axis=1)
        averaged = neighbour_average(window, mask_rows, first_row, 0, ROWS, COLS)
        columns = averaged.reshape(pixel_count, -1).astype(jnp.float32)
        inv_pattern = 1.0 / jnp.sqrt(lax.optimization_barrier(jnp.mean(columns * columns, axis=0)) + epsilon)
        products = jnp.einsum('kep,pm->kem', dictionary32, columns)
        scores = products / pixel_count * inv_entry[:, :, None] * inv_pattern[None, None, :]
        ranked = -jnp.sort(-scores, axis=1)[:, :TOP]
        return ranked.reshape(PANELS, TOP, ROWS_DEV, COLS)
    ranked_all = lax.map(score_rows, jnp.arange(block_count, dtype=jnp.int32))
    return jnp.moveaxis(ranked_all, 0, 2).reshape(PANELS, TOP, ROWS, COLS)
```

```python
import functools

import jax
import jax.numpy as jnp
import numpy as np
from jax import lax
from jax.experimental import pallas as pl
from jax.experimental.pallas import tpu as pltpu
from jax.sharding import PartitionSpec as P

PH = 60
NPIX = PH * PH
TOP = 4
epsilon = 1e-05
nlpar_scale = 2.0

GROUPS = 15
RUN = 240
RUN_PAD = 256
DEPTH = GROUPS * RUN_PAD
PITCH = 160
LEAD = 336
COLS_DEV = 128
ROWS_DEV = 8
TILES = 7
LANES = TILES * 256
HELD = LEAD + LANES
OFFSETS = tuple(PITCH * a + b for a in (-1, 0, 1) for b in (-1, 0, 1))
NT = (((1,), (1,)), ((), ()))
LIMIT = pltpu.CompilerParams(vmem_limit_bytes=62 << 20)


def tables():
    positions = np.arange(PH, dtype=np.float64)
    spread_px = PH / 8.0
    profile = np.exp(-((positions[:, None] - positions[None, :]) ** 2) / (2.0 * spread_px**2))
    k = profile / profile.sum(axis=1, keepdims=True)
    q = np.arange(RUN)
    d, low = (q // 16) * 4 + (q // 4) % 4, q % 4
    src_a, src_b = q // PH, q % PH
    same = low[:, None] == src_a[None, :]
    first = np.where(same, k[d[:, None], src_b[None, :]], 0.0)
    order = np.where(same & (d[:, None] == src_b[None, :]), 1.0, 0.0)
    e = (q // 16) * 4 + low
    d4 = (q // 4) % 4
    second = np.where(d4[:, None] == d4[None, :], k[e[:, None], e[None, :]], 0.0)
    bf = functools.partial(jnp.asarray, dtype=jnp.bfloat16)
    order_t = np.zeros((RUN, RUN_PAD))
    order_t[:, :RUN] = order.T
    return bf(np.concatenate([first, order])), bf(second), bf(np.eye(256)), bf(order_t)


def standardize_kernel(x_ref, k1_ref, k2_ref, eye_ref, m_ref, s_ref, xs, h, c):
    g = pl.program_id(0)
    for j in range(6):
        xs[pl.ds(j * 320, 320), :] = x_ref[pl.ds(j * 40, 40)].astype(jnp.float32).reshape(320, 128)
    h_at = pl.ds(pl.multiple_of(g * 16, 16), 16)
    for n in range(4):
        even = xs[pl.ds(2 * n, RUN, stride=8), :].astype(jnp.bfloat16)
        odd = xs[pl.ds(2 * n + 1, RUN, stride=8), :].astype(jnp.bfloat16)
        pair = jnp.concatenate([even, odd], axis=1)
        out = jnp.dot(k1_ref[...], pair, preferred_element_type=jnp.float32)
        h[n, :, h_at, :] = out[:RUN].astype(jnp.bfloat16).reshape(GROUPS, 16, 256)
        c[n, g] = out[RUN:].reshape(GROUPS, 16, 256)

    @pl.when(g == GROUPS - 1)
    def _():
        for n in range(4):
            def second(dc, carry):
                total, square = carry
                out = jnp.dot(k2_ref[...], h[n, dc], preferred_element_type=jnp.float32)
                corrected = c[n, :, dc] - out.reshape(GROUPS, 16, 256)
                c[n, :, dc] = corrected
                part = corrected.reshape(2 * GROUPS, 8, 256)
                return total + jnp.sum(part, axis=0), square + jnp.sum(part * part, axis=0)

            zero = jnp.zeros((8, 256), jnp.float32)
            total, square = lax.fori_loop(0, GROUPS, second, (zero, zero))
            mean = jnp.sum(total, axis=0, keepdims=True) / NPIX
            var = jnp.sum(square, axis=0, keepdims=True) / NPIX - mean * mean
            mask = jnp.concatenate([m_ref[2 * n : 2 * n + 1, :], m_ref[2 * n + 1 : 2 * n + 2, :]], axis=1)
            scale = mask.astype(jnp.float32) / jnp.sqrt(jnp.maximum(var, 0.0) + epsilon)
            shift = mean * scale

            def third(ge, carry):
                v = (c[n, ge].reshape(RUN, 256) * scale - shift).astype(jnp.bfloat16)
                v = jnp.concatenate([v, jnp.zeros((16, 256), jnp.bfloat16)], axis=0)
                out = lax.dot_general(eye_ref[...], v, NT, preferred_element_type=jnp.float32)
                at = pl.ds(pl.multiple_of(ge * RUN_PAD, RUN_PAD), RUN_PAD)
                s_ref[pl.ds(256 * n, 256), at] = out.astype(jnp.bfloat16)
                return carry

            lax.fori_loop(0, GROUPS, third, 0)


def standardize(patterns, scan_mask, k1, k2, eye):
    whole = lambda *dims: pl.BlockSpec(dims, lambda g: (0,) * len(dims))
    return pl.pallas_call(
        standardize_kernel,
        grid=(GROUPS,),
        in_specs=[
            pl.BlockSpec((RUN, ROWS_DEV, COLS_DEV), lambda g: (g, 0, 0)),
            whole(2 * RUN, RUN),
            whole(RUN, RUN),
            whole(256, 256),
            whole(ROWS_DEV, COLS_DEV),
        ],
        out_specs=whole(ROWS_DEV * COLS_DEV, DEPTH),
        out_shape=jax.ShapeDtypeStruct((ROWS_DEV * COLS_DEV, DEPTH), jnp.bfloat16),
        scratch_shapes=[
            pltpu.VMEM((RUN * 8, 128), jnp.float32),
            pltpu.VMEM((4, GROUPS, RUN, 256), jnp.bfloat16),
            pltpu.VMEM((4, GROUPS, GROUPS, 16, 256), jnp.float32),
        ],
        compiler_params=LIMIT,
        name="standardize",
    )(patterns, k1, k2, eye, scan_mask)


def prepare_kernel(d_ref, order_ref, o_ref):
    x = jnp.concatenate([d_ref[0].astype(jnp.float32), d_ref[1].astype(jnp.float32)], axis=0)
    inv = 1.0 / jnp.sqrt(jnp.sum(x * x, axis=1, keepdims=True) / NPIX + epsilon)
    hi = inv.astype(jnp.bfloat16).astype(jnp.float32)
    mid = (inv - hi).astype(jnp.bfloat16).astype(jnp.float32)
    low = inv - hi - mid
    xb = x.astype(jnp.bfloat16)
    for ge in range(GROUPS):
        run = xb[:, ge * RUN : (ge + 1) * RUN]
        out = jnp.dot(run, order_ref[...], preferred_element_type=jnp.float32)
        if ge == GROUPS - 1:
            lane = lax.broadcasted_iota(jnp.int32, out.shape, 1)
            for i, piece in enumerate((hi, mid, low)):
                out = jnp.where(lane == RUN + i, piece, out)
        o_ref[:, ge * RUN_PAD : (ge + 1) * RUN_PAD] = out.astype(jnp.bfloat16)


def prepare(dictionary, order_t):
    return pl.pallas_call(
        prepare_kernel,
        out_shape=jax.ShapeDtypeStruct((8, DEPTH), jnp.bfloat16),
        name="prepare",
    )(dictionary, order_t)


def row_start(scan_row):
    return LEAD + PITCH * scan_row


def gram_fields(st, f8):
    row_at = lax.broadcasted_iota(jnp.int32, (136, 128), 0)
    lane_at = lax.broadcasted_iota(jnp.int32, (136, 128), 1)
    slots = {}
    for kk in range(9):
        for low in range(min(kk + 1, 8)):
            slots.setdefault(OFFSETS[kk] - OFFSETS[low], []).append((kk, low))
    f8[...] = jnp.zeros_like(f8)

    def tile(t, carry):
        n0 = pl.multiple_of(t * 256, 256)
        rows = st[pl.ds(n0, LEAD + 256), :]
        cols = st[pl.ds(pl.multiple_of(n0 + LEAD, 16), 256), :]
        g = lax.dot_general(rows, cols, NT, preferred_element_type=jnp.float32)
        for half in range(2):
            lanes = g[:, half * 128 : (half + 1) * 128]
            for o, where_to in slots.items():
                first = LEAD + half * 128 - o
                start = min(first // 8 * 8, LEAD + 256 - 136)
                hit = row_at + (start - first) == lane_at
                value = jnp.sum(jnp.where(hit, lanes[start : start + 136], 0.0), axis=0, keepdims=True)
                at = pl.ds(pl.multiple_of(n0 + half * 128, 128), 128)
                for kk, low in where_to:
                    f8[kk, low : low + 1, at] = value
        return carry

    lax.fori_loop(0, TILES, tile, 0)


def usable_rows(nm_ref, u, first_row, first_col, all_rows, all_cols):
    u[...] = jnp.zeros_like(u)
    kk = lax.broadcasted_iota(jnp.int32, (8, 128), 0)
    kk = kk + (kk >= 4).astype(jnp.int32)
    down = (kk >= 3).astype(jnp.int32) + (kk >= 6).astype(jnp.int32) - 1
    right = kk - 3 * (down + 1) - 1
    col = lax.broadcasted_iota(jnp.int32, (8, 128), 1) + first_col + right
    col_ok = (col >= 0) & (col < all_cols)
    for r in range(ROWS_DEV):
        row = down + (first_row + r)
        ok = (row >= 0) & (row < all_rows) & col_ok & (nm_ref[:, r, :] == 1)
        at = PITCH * (r + 1) + 16
        u[:, at : at + 128] = ok.astype(jnp.float32)


def weigh(f8, u, w):
    def turn(x, off):
        return x if off == 0 else pltpu.roll(x, (-off) % LANES, 1)

    n = f8[0, 0:1, :]
    centre = f8[4]
    placed = {4: centre}
    for kk in (0, 1, 2, 3, 5, 6, 7, 8):
        placed[kk] = turn(f8[kk], OFFSETS[kk])
    last = turn(jnp.broadcast_to(n, (8, LANES)), OFFSETS[8])[0:1]
    own = [placed[kk][kk : kk + 1] if kk < 8 else last for kk in range(9)]
    den = jnp.ones((1, LANES), jnp.float32)
    weights = []
    for kk in range(9):
        if kk == 4:
            value = jnp.ones((1, LANES), jnp.float32)
        else:
            dot = centre[kk : kk + 1] if kk < 4 else placed[kk][4:5]
            distance = (n + own[kk] - 2.0 * dot) / NPIX
            slot = kk if kk < 4 else kk - 1
            value = jnp.where(u[slot : slot + 1, :] > 0.5, jnp.exp(-distance / nlpar_scale), 0.0)
            den = den + value
        weights.append(value)
        w[kk : kk + 1, :] = value
    lows = w[0:8, :]
    quad = jnp.zeros((1, LANES), jnp.float32)
    for kk in range(9):
        part = 2.0 * jnp.sum(lows * placed[kk], axis=0, keepdims=True)
        self_term = weights[kk] * own[kk]
        part = part - self_term if kk < 8 else part + self_term
        quad = quad + weights[kk] * part
    square = jnp.maximum(quad, 0.0) / (den * den) / NPIX
    w[9:10, :] = 1.0 / (jnp.sqrt(square + epsilon) * den * NPIX)


def spread(w, wc, we):
    lane = lax.broadcasted_iota(jnp.int32, (16, 128), 1)
    edge = jnp.zeros((16, 128), jnp.float32)
    kinds = lax.broadcasted_iota(jnp.int32, (16, 128), 0)
    left = (kinds == 0) | (kinds == 3) | (kinds == 6)
    right = (kinds == 2) | (kinds == 5) | (kinds == 8)
    for r in range(ROWS_DEV):
        at = PITCH * (r + 1) + 16
        here = w[:, at : at + 128]
        before = w[:, at + 1 : at + 129]
        after = w[:, at - 1 : at + 127]
        wc[r] = jnp.where(left, before, jnp.where(right, after, here))
        R = r + 1
        edge = jnp.where(lane == 2 * R, pltpu.roll(here, 2 * R, 1), edge)
        edge = jnp.where(lane == 2 * R + 1, pltpu.roll(here, 2 * R + 2, 1), edge)
    odd = lane[0:1] % 2 == 1
    for i in range(3):
        we[i : i + 1, :] = jnp.where(odd, edge[3 * i + 2 : 3 * i + 3], edge[3 * i : 3 * i + 1])


def edge_rows(st, et):
    for R in range(10):
        top = row_start(R)
        tile = st[pl.ds(top, 16), :].astype(jnp.float32)
        et[2 * R : 2 * R + 1, :] = tile[15:16]
        tile = st[pl.ds(top + 144, 16), :].astype(jnp.float32)
        et[2 * R + 1 : 2 * R + 2, :] = tile[0:1]
    et[20:32, :] = jnp.zeros((12, DEPTH), jnp.float32)


def products(d_ref, st, et, p):
    def pair(i, carry):
        a = pl.multiple_of(LEAD + 16 + 2 * PITCH * i, 16)
        b = pl.multiple_of(LEAD + 16 + 2 * PITCH * i + PITCH, 16)
        rows = jnp.concatenate([st[pl.ds(a, 128), :], st[pl.ds(b, 128), :]], axis=0)
        out = lax.dot_general(d_ref[...], rows, NT, preferred_element_type=jnp.float32)
        p[2 * i] = out[:, :128]
        p[2 * i + 1] = out[:, 128:]
        return carry

    lax.fori_loop(0, 5, pair, 0)
    edge = et[...].astype(jnp.bfloat16)
    edge = jnp.concatenate([edge, jnp.zeros((96, DEPTH), jnp.bfloat16)], axis=0)
    p[10] = lax.dot_general(d_ref[...], edge, NT, preferred_element_type=jnp.float32)


def entry_norms(d_ref, inv):
    tail = d_ref[:, DEPTH - 128 :].astype(jnp.float32)
    at = RUN - 128
    value = tail[:, at : at + 1] + tail[:, at + 1 : at + 2] + tail[:, at + 2 : at + 3]
    inv[...] = jnp.broadcast_to(value, inv.shape)


def edge_mix(p, we):
    def step(k, carry):
        at = pl.ds(pl.multiple_of(k * 8, 8), 8)
        e = p[10, at, :]
        mix = e * we[1:2, :] + pltpu.roll(e, 2, 1) * we[0:1, :] + pltpu.roll(e, 126, 1) * we[2:3, :]
        p[10, at, :] = mix
        return carry

    lax.fori_loop(0, 128, step, 0, unroll=8)


def best_scores(p, inv, wc, o_ref):
    lane = lax.broadcasted_iota(jnp.int32, (8, 128), 1)
    first, last = lane == 0, lane == 127
    for r in range(ROWS_DEV):
        wt = [jnp.broadcast_to(wc[r, kk : kk + 1, :], (8, 128)) for kk in range(9)]
        R = r + 1

        def step(k, best):
            at = pl.ds(pl.multiple_of(k * 8, 8), 8)
            up, mid, down = p[r, at, :], p[r + 1, at, :], p[r + 2, at, :]
            edge = pltpu.roll(p[10, at, :], 127 - 2 * R, 1)
            left = up * wt[0] + mid * wt[3] + down * wt[6]
            right = up * wt[2] + mid * wt[5] + down * wt[8]
            here = up * wt[1] + mid + down * wt[7]
            left = jnp.where(last, edge, left)
            right = jnp.where(first, edge, right)
            v = (here + pltpu.roll(left, 1, 1) + pltpu.roll(right, 127, 1)) * inv[at, :]
            b0, b1, b2, b3 = best
            n0, v = jnp.maximum(b0, v), jnp.minimum(b0, v)
            n1, v = jnp.maximum(b1, v), jnp.minimum(b1, v)
            n2, v = jnp.maximum(b2, v), jnp.minimum(b2, v)
            return n0, n1, n2, jnp.maximum(b3, v)

        low = jnp.full((8, 128), -jnp.inf, jnp.float32)
        best = lax.fori_loop(0, 128, step, (low, low, low, low), unroll=4)
        for shift in (6, 7):
            other = [pltpu.roll(b, shift, 0) for b in best]
            m = [jnp.maximum(best[i], other[3 - i]) for i in range(4)]
            h0, l0 = jnp.maximum(m[0], m[2]), jnp.minimum(m[0], m[2])
            h1, l1 = jnp.maximum(m[1], m[3]), jnp.minimum(m[1], m[3])
            best = (jnp.maximum(h0, h1), jnp.minimum(h0, h1), jnp.maximum(l0, l1), jnp.minimum(l0, l1))
        scale = wc[r, 9:10, :]
        for j in range(TOP):
            o_ref[0, j, r : r + 1, :] = best[j][0:1] * scale
            o_ref[1, j, r : r + 1, :] = best[j][4:5] * scale


def index_kernel(rows_axis, cols_axis, s_hbm, up_hbm, down_hbm, left_hbm, right_hbm, d_ref, nm_ref, o_ref,
                 st, et, p, f8, u, w, wc, we, inv, sem):
    copies = []
    for r in range(ROWS_DEV):
        copies.append((s_hbm.at[pl.ds(128 * r, 128), :], st.at[pl.ds(row_start(r + 1) + 16, 128), :]))
    copies.append((up_hbm, st.at[pl.ds(row_start(0) + 16, 128), :]))
    copies.append((down_hbm, st.at[pl.ds(row_start(9) + 16, 128), :]))
    for R in range(10):
        copies.append((left_hbm.at[R], st.at[pl.ds(row_start(R), 16), :]))
        copies.append((right_hbm.at[R], st.at[pl.ds(row_start(R) + 144, 16), :]))
    started = [pltpu.make_async_copy(a, b, sem.at[i]) for i, (a, b) in enumerate(copies)]
    for copy in started:
        copy.start()
    st[pl.ds(0, LEAD), :] = jnp.zeros((LEAD, DEPTH), jnp.bfloat16)
    st[pl.ds(LEAD + 10 * PITCH, LANES - 10 * PITCH), :] = jnp.zeros((LANES - 10 * PITCH, DEPTH), jnp.bfloat16)
    first_row = lax.axis_index(rows_axis) * ROWS_DEV
    first_col = lax.axis_index(cols_axis) * COLS_DEV
    usable_rows(nm_ref, u, first_row, first_col, lax.axis_size(rows_axis) * ROWS_DEV, lax.axis_size(cols_axis) * COLS_DEV)
    for copy in started:
        copy.wait()
    w[...] = jnp.zeros_like(w)
    gram_fields(st, f8)
    weigh(f8, u, w)
    spread(w, wc, we)
    edge_rows(st, et)
    products(d_ref, st, et, p)
    entry_norms(d_ref, inv)
    edge_mix(p, we)
    best_scores(p, inv, wc, o_ref)


INDEX_SCRATCH = [
    pltpu.VMEM((HELD, DEPTH), jnp.bfloat16),
    pltpu.VMEM((32, DEPTH), jnp.float32),
    pltpu.VMEM((11, 1024, 128), jnp.float32),
    pltpu.VMEM((9, 8, LANES), jnp.float32),
    pltpu.VMEM((8, LANES), jnp.float32),
    pltpu.VMEM((16, LANES), jnp.float32),
    pltpu.VMEM((8, 16, 128), jnp.float32),
    pltpu.VMEM((8, 128), jnp.float32),
    pltpu.VMEM((1024, 128), jnp.float32),
]


def index_patterns(s, up, down, left, right, d, neighbour_mask):
    anywhere = pl.BlockSpec(memory_space=pl.ANY)
    vmem = pl.BlockSpec(memory_space=pltpu.VMEM)
    return pl.pallas_call(
        functools.partial(index_kernel, "strip", "dict"),
        in_specs=[anywhere] * 5 + [vmem, vmem],
        out_specs=vmem,
        out_shape=jax.ShapeDtypeStruct((2, TOP, ROWS_DEV, COLS_DEV), jnp.float32),
        scratch_shapes=INDEX_SCRATCH + [pltpu.SemaphoreType.DMA((30,))],
        compiler_params=LIMIT,
        name="index",
    )(s, up, down, left, right, d, neighbour_mask)


def gather_entries(mine):
    copies = jnp.broadcast_to(mine, (lax.axis_size("dict"), *mine.shape))
    grouped = lax.all_to_all(copies, "dict", split_axis=0, concat_axis=0, tiled=True)
    return lax.all_gather(grouped.reshape(-1, DEPTH), "strip", axis=0, tiled=True)


def shift(value, axis, step):
    count = lax.axis_size(axis)
    return lax.ppermute(value, axis, [(i, (i + step) % count) for i in range(count)])


def on_device(patterns, scan_mask, neighbour_mask, dictionary):
    k1, k2, eye, order_t = tables()
    d = gather_entries(prepare(dictionary, order_t))
    s = standardize(patterns, scan_mask, k1, k2, eye)
    up = shift(s[-128:], "strip", 1)
    down = shift(s[:128], "strip", -1)
    rows = jnp.concatenate([up[None], s.reshape(8, 128, DEPTH), down[None]], axis=0)
    left = shift(rows[:, 112:], "dict", 1)
    right = shift(rows[:, :16], "dict", -1)
    return index_patterns(s, up, down, left, right, d, neighbour_mask)


def solution(mesh):
    in_specs = (
        P(None, "strip", "dict"),
        P("strip", "dict"),
        P(None, "strip", "dict"),
        P(None, ("strip", "dict"), None),
    )
    out_specs = P(None, None, "strip", "dict")
    return jax.shard_map(
        on_device, mesh=mesh, in_specs=in_specs, out_specs=out_specs, check_vma=False
    )
```

```python
import functools

import jax
import jax.numpy as jnp
import numpy as np
from jax import lax
from jax.experimental import pallas as pl
from jax.experimental.pallas import tpu as pltpu
from jax.sharding import PartitionSpec as P

PH = 60
NPIX = PH * PH
TOP = 4
epsilon = 1e-05
nlpar_scale = 2.0

GROUPS = 15
RUN = 240
RUN_PAD = 256
DEPTH = GROUPS * RUN_PAD
PITCH = 160
LEAD = 336
COLS_DEV = 128
ROWS_DEV = 8
TILES = 7
LANES = TILES * 256
HELD = LEAD + LANES
OFFSETS = tuple(PITCH * a + b for a in (-1, 0, 1) for b in (-1, 0, 1))
NT = (((1,), (1,)), ((), ()))


def tables():
    positions = np.arange(PH, dtype=np.float64)
    spread_px = PH / 8.0
    profile = np.exp(-((positions[:, None] - positions[None, :]) ** 2) / (2.0 * spread_px**2))
    k = profile / profile.sum(axis=1, keepdims=True)
    q = np.arange(RUN)
    d, low = (q // 16) * 4 + (q // 4) % 4, q % 4
    src_a, src_b = q // PH, q % PH
    same = low[:, None] == src_a[None, :]
    first = np.where(same, k[d[:, None], src_b[None, :]], 0.0)
    order = np.where(same & (d[:, None] == src_b[None, :]), 1.0, 0.0)
    e = (q // 16) * 4 + low
    d4 = (q // 4) % 4
    second = np.where(d4[:, None] == d4[None, :], k[e[:, None], e[None, :]], 0.0)
    bf = functools.partial(jnp.asarray, dtype=jnp.bfloat16)
    order_t = np.zeros((RUN, RUN_PAD))
    order_t[:, :RUN] = order.T
    return bf(np.concatenate([first, order])), bf(second), bf(np.eye(256)), bf(order_t)


def prepare(d_ref, order_ref, own):
    x = jnp.concatenate([d_ref[0].astype(jnp.float32), d_ref[1].astype(jnp.float32)], axis=0)
    inv = 1.0 / jnp.sqrt(jnp.sum(x * x, axis=1, keepdims=True) / NPIX + epsilon)
    hi = inv.astype(jnp.bfloat16).astype(jnp.float32)
    mid = (inv - hi).astype(jnp.bfloat16).astype(jnp.float32)
    low = inv - hi - mid
    xb = x.astype(jnp.bfloat16)
    for ge in range(GROUPS):
        run = xb[:, ge * RUN : (ge + 1) * RUN]
        out = jnp.dot(run, order_ref[...], preferred_element_type=jnp.float32)
        if ge == GROUPS - 1:
            lane = lax.broadcasted_iota(jnp.int32, out.shape, 1)
            for i, piece in enumerate((hi, mid, low)):
                out = jnp.where(lane == RUN + i, piece, out)
        own[:, ge * RUN_PAD : (ge + 1) * RUN_PAD] = out


def first_pass(g, x_ref, k1_ref, xs, h, c):
    for j in range(6):
        xs[pl.ds(j * 320, 320), :] = x_ref[pl.ds(j * 40, 40)].astype(jnp.float32).reshape(320, 128)
    h_at = pl.ds(pl.multiple_of(g * 16, 16), 16)
    for n in range(4):
        even = xs[pl.ds(2 * n, RUN, stride=8), :].astype(jnp.bfloat16)
        odd = xs[pl.ds(2 * n + 1, RUN, stride=8), :].astype(jnp.bfloat16)
        pair = jnp.concatenate([even, odd], axis=1)
        out = jnp.dot(k1_ref[...], pair, preferred_element_type=jnp.float32)
        h[n, :, h_at, :] = out[:RUN].astype(jnp.bfloat16).reshape(GROUPS, 16, 256)
        c[n, g] = out[RUN:].reshape(GROUPS, 16, 256)


def second_pass(n, k2_ref, eye_ref, m_ref, h, c, st):
    def second(dc, carry):
        total, square = carry
        out = jnp.dot(k2_ref[...], h[n, dc], preferred_element_type=jnp.float32)
        corrected = c[n, :, dc] - out.reshape(GROUPS, 16, 256)
        c[n, :, dc] = corrected
        part = corrected.reshape(2 * GROUPS, 8, 256)
        return total + jnp.sum(part, axis=0), square + jnp.sum(part * part, axis=0)

    zero = jnp.zeros((8, 256), jnp.float32)
    total, square = lax.fori_loop(0, GROUPS, second, (zero, zero))
    mean = jnp.sum(total, axis=0, keepdims=True) / NPIX
    var = jnp.sum(square, axis=0, keepdims=True) / NPIX - mean * mean
    mask = jnp.concatenate([m_ref[2 * n : 2 * n + 1, :], m_ref[2 * n + 1 : 2 * n + 2, :]], axis=1)
    scale = mask.astype(jnp.float32) / jnp.sqrt(jnp.maximum(var, 0.0) + epsilon)
    shift = mean * scale

    def third(ge, carry):
        v = (c[n, ge].reshape(RUN, 256) * scale - shift).astype(jnp.bfloat16)
        v = jnp.concatenate([v, jnp.zeros((16, 256), jnp.bfloat16)], axis=0)
        out = lax.dot_general(eye_ref[...], v, NT, preferred_element_type=jnp.float32)
        out = out.astype(jnp.bfloat16)
        at = pl.ds(pl.multiple_of(ge * RUN_PAD, RUN_PAD), RUN_PAD)
        st[pl.ds(own_start(2 * n), 128), at] = out[:128]
        st[pl.ds(own_start(2 * n + 1), 128), at] = out[128:]
        return carry

    lax.fori_loop(0, GROUPS, third, 0)


def row_start(scan_row):
    return LEAD + PITCH * scan_row


def own_start(r):
    return row_start(r + 1) + 16


def gram_fields(st, f8):
    row_at = lax.broadcasted_iota(jnp.int32, (136, 128), 0)
    lane_at = lax.broadcasted_iota(jnp.int32, (136, 128), 1)
    slots = {}
    for kk in range(9):
        for low in range(min(kk + 1, 8)):
            slots.setdefault(OFFSETS[kk] - OFFSETS[low], []).append((kk, low))
    f8[...] = jnp.zeros_like(f8)

    def tile(t, carry):
        n0 = pl.multiple_of(t * 256, 256)
        rows = st[pl.ds(n0, LEAD + 256), :]
        cols = st[pl.ds(pl.multiple_of(n0 + LEAD, 16), 256), :]
        g = lax.dot_general(rows, cols, NT, preferred_element_type=jnp.float32)
        for half in range(2):
            lanes = g[:, half * 128 : (half + 1) * 128]
            for o, where_to in slots.items():
                first = LEAD + half * 128 - o
                start = min(first // 8 * 8, LEAD + 256 - 136)
                hit = row_at + (start - first) == lane_at
                value = jnp.sum(jnp.where(hit, lanes[start : start + 136], 0.0), axis=0, keepdims=True)
                at = pl.ds(pl.multiple_of(n0 + half * 128, 128), 128)
                for kk, low in where_to:
                    f8[kk, low : low + 1, at] = value
        return carry

    lax.fori_loop(0, TILES, tile, 0)


def usable_rows(nm_ref, u, first_row, first_col, all_rows, all_cols):
    u[...] = jnp.zeros_like(u)
    kk = lax.broadcasted_iota(jnp.int32, (8, 128), 0)
    kk = kk + (kk >= 4).astype(jnp.int32)
    down = (kk >= 3).astype(jnp.int32) + (kk >= 6).astype(jnp.int32) - 1
    right = kk - 3 * (down + 1) - 1
    col = lax.broadcasted_iota(jnp.int32, (8, 128), 1) + first_col + right
    col_ok = (col >= 0) & (col < all_cols)
    for r in range(ROWS_DEV):
        row = down + (first_row + r)
        ok = (row >= 0) & (row < all_rows) & col_ok & (nm_ref[:, r, :] == 1)
        at = PITCH * (r + 1) + 16
        u[:, at : at + 128] = ok.astype(jnp.float32)


def weigh(f8, u, w):
    def turn(x, off):
        return x if off == 0 else pltpu.roll(x, (-off) % LANES, 1)

    n = f8[0, 0:1, :]
    centre = f8[4]
    placed = {4: centre}
    for kk in (0, 1, 2, 3, 5, 6, 7, 8):
        placed[kk] = turn(f8[kk], OFFSETS[kk])
    last = turn(jnp.broadcast_to(n, (8, LANES)), OFFSETS[8])[0:1]
    own = [placed[kk][kk : kk + 1] if kk < 8 else last for kk in range(9)]
    den = jnp.ones((1, LANES), jnp.float32)
    weights = []
    for kk in range(9):
        if kk == 4:
            value = jnp.ones((1, LANES), jnp.float32)
        else:
            dot = centre[kk : kk + 1] if kk < 4 else placed[kk][4:5]
            distance = (n + own[kk] - 2.0 * dot) / NPIX
            slot = kk if kk < 4 else kk - 1
            value = jnp.where(u[slot : slot + 1, :] > 0.5, jnp.exp(-distance / nlpar_scale), 0.0)
            den = den + value
        weights.append(value)
        w[kk : kk + 1, :] = value
    lows = w[0:8, :]
    quad = jnp.zeros((1, LANES), jnp.float32)
    for kk in range(9):
        part = 2.0 * jnp.sum(lows * placed[kk], axis=0, keepdims=True)
        self_term = weights[kk] * own[kk]
        part = part - self_term if kk < 8 else part + self_term
        quad = quad + weights[kk] * part
    square = jnp.maximum(quad, 0.0) / (den * den) / NPIX
    w[9:10, :] = 1.0 / (jnp.sqrt(square + epsilon) * den * NPIX)


def spread(w, wc, we):
    lane = lax.broadcasted_iota(jnp.int32, (16, 128), 1)
    edge = jnp.zeros((16, 128), jnp.float32)
    kinds = lax.broadcasted_iota(jnp.int32, (16, 128), 0)
    left = (kinds == 0) | (kinds == 3) | (kinds == 6)
    right = (kinds == 2) | (kinds == 5) | (kinds == 8)
    for r in range(ROWS_DEV):
        at = PITCH * (r + 1) + 16
        here = w[:, at : at + 128]
        before = w[:, at + 1 : at + 129]
        after = w[:, at - 1 : at + 127]
        wc[r] = jnp.where(left, before, jnp.where(right, after, here))
        R = r + 1
        edge = jnp.where(lane == 2 * R, pltpu.roll(here, 2 * R, 1), edge)
        edge = jnp.where(lane == 2 * R + 1, pltpu.roll(here, 2 * R + 2, 1), edge)
    odd = lane[0:1] % 2 == 1
    for i in range(3):
        we[i : i + 1, :] = jnp.where(odd, edge[3 * i + 2 : 3 * i + 3], edge[3 * i : 3 * i + 1])


def own_edges(st, et, eout):
    for r in range(ROWS_DEV):
        top = own_start(r)
        et[r : r + 1, :] = st[pl.ds(top, 16), :].astype(jnp.float32)[0:1]
        et[16 + r : 17 + r, :] = st[pl.ds(top + 112, 16), :].astype(jnp.float32)[15:16]
    et[8:16, :] = jnp.zeros((8, DEPTH), jnp.float32)
    et[24:32, :] = jnp.zeros((8, DEPTH), jnp.float32)
    eout[0] = et[0:16, :].astype(jnp.bfloat16)
    eout[1] = et[16:32, :].astype(jnp.bfloat16)


def place_edges(R, left, right, st, et):
    et[2 * R : 2 * R + 1, :] = left
    et[2 * R + 1 : 2 * R + 2, :] = right
    st[pl.ds(row_start(R), 16), :] = jnp.broadcast_to(left, (16, DEPTH)).astype(jnp.bfloat16)
    st[pl.ds(row_start(R) + 144, 16), :] = jnp.broadcast_to(right, (16, DEPTH)).astype(jnp.bfloat16)


def inner_edges(ein, st, et, cout):
    left, right = ein[0].astype(jnp.float32), ein[1].astype(jnp.float32)
    row = lax.broadcasted_iota(jnp.int32, (16, DEPTH), 0)
    for i, r in enumerate((0, ROWS_DEV - 1)):
        both = jnp.where(row == 0, left[r : r + 1], right[r : r + 1])
        cout[i] = both.astype(jnp.bfloat16)
    for r in range(ROWS_DEV):
        place_edges(r + 1, left[r : r + 1], right[r : r + 1], st, et)


def corner_edges(cin, st, et):
    for i, R in enumerate((0, ROWS_DEV + 1)):
        both = cin[i].astype(jnp.float32)
        place_edges(R, both[0:1], both[1:2], st, et)
    et[20:32, :] = jnp.zeros((12, DEPTH), jnp.float32)


def pair_product(d, st, p, i, j):
    a = pl.multiple_of(LEAD + 16 + PITCH * i, 16)
    b = pl.multiple_of(LEAD + 16 + PITCH * j, 16)
    rows = jnp.concatenate([st[pl.ds(a, 128), :], st[pl.ds(b, 128), :]], axis=0)
    out = lax.dot_general(d[...].reshape(1024, DEPTH), rows, NT, preferred_element_type=jnp.float32)
    p[i] = out[:, :128]
    p[j] = out[:, 128:]


def own_products(d, st, p):
    def pair(i, carry):
        pair_product(d, st, p, 2 * i + 1, 2 * i + 2)
        return carry

    lax.fori_loop(0, ROWS_DEV // 2, pair, 0)


def edge_products(d, st, et, p):
    pair_product(d, st, p, 0, ROWS_DEV + 1)
    edge = et[...].astype(jnp.bfloat16)
    edge = jnp.concatenate([edge, jnp.zeros((96, DEPTH), jnp.bfloat16)], axis=0)
    p[10] = lax.dot_general(d[...].reshape(1024, DEPTH), edge, NT, preferred_element_type=jnp.float32)


def entry_norms(d, inv):
    tail = d[:, :, :, DEPTH - 128 :].reshape(1024, 128).astype(jnp.float32)
    at = RUN - 128
    value = tail[:, at : at + 1] + tail[:, at + 1 : at + 2] + tail[:, at + 2 : at + 3]
    inv[...] = jnp.broadcast_to(value, inv.shape)


def edge_mix(p, we):
    def step(k, carry):
        at = pl.ds(pl.multiple_of(k * 8, 8), 8)
        e = p[10, at, :]
        mix = e * we[1:2, :] + pltpu.roll(e, 2, 1) * we[0:1, :] + pltpu.roll(e, 126, 1) * we[2:3, :]
        p[10, at, :] = mix
        return carry

    lax.fori_loop(0, 128, step, 0, unroll=8)


def best_scores(p, inv, wc, o_ref):
    lane = lax.broadcasted_iota(jnp.int32, (8, 128), 1)
    first, last = lane == 0, lane == 127
    for r in range(ROWS_DEV):
        wt = [jnp.broadcast_to(wc[r, kk : kk + 1, :], (8, 128)) for kk in range(9)]
        R = r + 1

        def step(k, best):
            at = pl.ds(pl.multiple_of(k * 8, 8), 8)
            up, mid, down = p[r, at, :], p[r + 1, at, :], p[r + 2, at, :]
            edge = pltpu.roll(p[10, at, :], 127 - 2 * R, 1)
            left = up * wt[0] + mid * wt[3] + down * wt[6]
            right = up * wt[2] + mid * wt[5] + down * wt[8]
            here = up * wt[1] + mid + down * wt[7]
            left = jnp.where(last, edge, left)
            right = jnp.where(first, edge, right)
            v = (here + pltpu.roll(left, 1, 1) + pltpu.roll(right, 127, 1)) * inv[at, :]
            b0, b1, b2, b3 = best
            n0, v = jnp.maximum(b0, v), jnp.minimum(b0, v)
            n1, v = jnp.maximum(b1, v), jnp.minimum(b1, v)
            n2, v = jnp.maximum(b2, v), jnp.minimum(b2, v)
            return n0, n1, n2, jnp.maximum(b3, v)

        low = jnp.full((8, 128), -jnp.inf, jnp.float32)
        best = lax.fori_loop(0, 128, step, (low, low, low, low), unroll=4)
        for shift in (6, 7):
            other = [pltpu.roll(b, shift, 0) for b in best]
            m = [jnp.maximum(best[i], other[3 - i]) for i in range(4)]
            h0, l0 = jnp.maximum(m[0], m[2]), jnp.minimum(m[0], m[2])
            h1, l1 = jnp.maximum(m[1], m[3]), jnp.minimum(m[1], m[3])
            best = (jnp.maximum(h0, h1), jnp.minimum(h0, h1), jnp.maximum(l0, l1), jnp.minimum(l0, l1))
        scale = wc[r, 9:10, :]
        for j in range(TOP):
            o_ref[0, j, r : r + 1, :] = best[j][0:1] * scale
            o_ref[1, j, r : r + 1, :] = best[j][4:5] * scale


def send(src, dst, sems, i, device):
    return pltpu.make_async_remote_copy(
        src_ref=src,
        dst_ref=dst,
        send_sem=sems.at[0, i],
        recv_sem=sems.at[1, i],
        device_id=device,
        device_id_type=pl.DeviceIdType.MESH,
    )


COPIES = 48


def index_kernel(x_hbm, k1_ref, k2_ref, eye_ref, order_ref, m_ref, nm_ref, dict_ref, o_ref,
                 xbuf, xs, h, c, d, own, sib, st, eout, ein, cout, cin,
                 et, p, f8, u, w, wc, we, inv, xsem, sems):
    strip, slot = lax.axis_index("strip"), lax.axis_index("dict")
    core, zl = slot % 2, slot // 2
    zh, ix, iy = strip // 16, (strip // 4) % 4, strip % 4
    iz = zh * 2 + zl

    def chip(x, y, z):
        x, y, z = x % 4, y % 4, z % 4
        return ((z // 2) * 16 + x * 4 + y, (z % 2) * 2 + core)

    sibling = (strip, zl * 2 + (1 - core))
    x_up, x_down = chip(ix + 1, iy, iz), chip(ix + 3, iy, iz)
    y_up, y_down = chip(ix, iy + 1, iz), chip(ix, iy + 3, iz)
    z_up, z_down = chip(ix, iy, iz + 1), chip(ix, iy, iz + 3)
    row_up, row_down = ((strip + 31) % 32, slot), ((strip + 1) % 32, slot)
    col_left, col_right = (strip, (slot + 3) % 4), (strip, (slot + 1) % 4)

    def fetch(g, at):
        rows = pl.ds(pl.multiple_of(g * RUN, RUN), RUN)
        return pltpu.make_async_copy(x_hbm.at[rows], xbuf.at[at], xsem.at[at])

    fetch(0, 0).start()
    peers = (sibling, x_up, x_down, y_up, y_down, z_up, z_down, row_up, row_down, col_left, col_right)
    barrier = pltpu.get_barrier_semaphore()
    for peer in peers:
        pl.semaphore_signal(barrier, inc=1, device_id=peer, device_id_type=pl.DeviceIdType.MESH)
    prepare(dict_ref, order_ref, own)
    pl.semaphore_wait(barrier, len(peers))
    exchange = send(own, sib, sems, 0, sibling)
    exchange.start()

    base = pl.multiple_of(core * 1920, 128)
    half = pl.ds(base, 1920)
    part_a = pl.ds(base, 1024)
    part_b = pl.ds(pl.multiple_of(base + 1024, 128), 896)
    xu, xd, yu, yd, zu, zd = [(v % 4) for v in (ix + 1, ix + 3, iy + 1, iy + 3, iz + 1, iz + 3)]

    def same(ref, i, device):
        return send(ref, ref, sems, i, device)

    def rows_of(y):
        return pl.ds(pl.multiple_of(y * 16, 16), 16)

    upper, lower = pl.ds(0, 32), pl.ds(32, 32)
    y_first = [same(d.at[ix, iz, rows_of(iy), half], 1, y_up), same(d.at[ix, iz, rows_of(iy), half], 2, y_down)]
    y_second = [same(d.at[ix, iz, rows_of(yd), part_a], 3, y_up), same(d.at[ix, iz, rows_of(yu), part_b], 4, y_down)]
    mid_first = [
        same(d.at[ix, iz, :, part_a], 5, z_up),
        same(d.at[ix, iz, :, part_a], 6, z_down),
        same(d.at[ix, iz, :, part_b], 7, x_up),
        same(d.at[ix, iz, :, part_b], 8, x_down),
    ]
    mid_second = [
        same(d.at[ix, zd, upper, part_a], 9, z_up),
        same(d.at[ix, zu, lower, part_a], 10, z_down),
        same(d.at[xd, iz, upper, part_b], 11, x_up),
        same(d.at[xu, iz, lower, part_b], 12, x_down),
    ]
    last_first = [
        same(d.at[ix, :, :, part_a], 13, x_up),
        same(d.at[ix, :, :, part_a], 14, x_down),
        same(d.at[:, iz, :, part_b], 15, z_up),
        same(d.at[:, iz, :, part_b], 16, z_down),
        same(d.at[ix, :, :, part_a], 17, sibling),
        same(d.at[:, iz, :, part_b], 18, sibling),
    ]
    first_two, last_two = pl.ds(0, 2), pl.ds(2, 2)
    last_second = [
        same(d.at[xd, first_two, :, part_a], 19, x_up),
        same(d.at[xu, last_two, :, part_a], 20, x_down),
        same(d.at[first_two, zd, :, part_b], 21, z_up),
        same(d.at[last_two, zu, :, part_b], 22, z_down),
        same(d.at[xd, :, :, part_a], 23, sibling),
        same(d.at[xu, :, :, part_a], 24, sibling),
        same(d.at[:, zd, :, part_b], 25, sibling),
        same(d.at[:, zu, :, part_b], 26, sibling),
    ]
    xo, zo = (ix + 2) % 4, (iz + 2) % 4
    final = [
        same(d.at[xo, :, :, part_a], 27, sibling),
        same(d.at[:, zo, :, part_b], 28, sibling),
    ]

    def start(copies):
        for copy in copies:
            copy.start()

    def arrive(copies):
        for copy in copies:
            copy.wait_recv()

    def begin():
        exchange.wait_recv()
        mine, other = own[:, half], sib[:, half]
        first = core == 0
        both = jnp.concatenate([jnp.where(first, mine, other), jnp.where(first, other, mine)], axis=0)
        d[ix, iz, rows_of(iy), half] = both.astype(jnp.bfloat16)
        start(y_first)

    def forward(arrived, following):
        def act():
            arrive(arrived)
            start(following)
        return act

    events = {
        1: begin,
        3: forward(y_first, y_second),
        5: forward(y_second, mid_first),
        8: forward(mid_first, mid_second),
        10: forward(mid_second, last_first),
    }
    st[pl.ds(0, LEAD), :] = jnp.zeros((LEAD, DEPTH), jnp.bfloat16)
    tail = LANES - 10 * PITCH
    st[pl.ds(LEAD + 10 * PITCH, tail), :] = jnp.zeros((tail, DEPTH), jnp.bfloat16)
    w[...] = jnp.zeros_like(w)
    usable_rows(nm_ref, u, strip * ROWS_DEV, slot * COLS_DEV, 32 * ROWS_DEV, 4 * COLS_DEV)

    def chunk(g, carry):
        at = g % 2

        @pl.when(g + 1 < GROUPS)
        def _():
            fetch(g + 1, 1 - at).start()

        fetch(g, at).wait()
        first_pass(g, xbuf.at[at], k1_ref, xs, h, c)
        for when, act in events.items():
            pl.when(g == when)(act)
        return carry

    lax.fori_loop(0, GROUPS, chunk, 0)

    row_copies = [
        send(st.at[pl.ds(own_start(7), 128), :], st.at[pl.ds(own_start(-1), 128), :], sems, 29, row_down),
        send(st.at[pl.ds(own_start(0), 128), :], st.at[pl.ds(own_start(8), 128), :], sems, 30, row_up),
    ]
    edge_copies = [
        send(eout.at[0], ein.at[1], sems, 31, col_left),
        send(eout.at[1], ein.at[0], sems, 32, col_right),
    ]
    corner_copies = [
        send(cout.at[0], cin.at[1], sems, 33, row_up),
        send(cout.at[1], cin.at[0], sems, 34, row_down),
    ]
    second_pass(3, k2_ref, eye_ref, m_ref, h, c, st)
    row_copies[0].start()
    second_pass(0, k2_ref, eye_ref, m_ref, h, c, st)
    row_copies[1].start()
    forward(last_first, last_second)()
    second_pass(1, k2_ref, eye_ref, m_ref, h, c, st)
    second_pass(2, k2_ref, eye_ref, m_ref, h, c, st)
    own_edges(st, et, eout)
    start(edge_copies)
    forward(last_second, final)()
    arrive(edge_copies)
    inner_edges(ein, st, et, cout)
    start(corner_copies)
    arrive(final)
    entry_norms(d, inv)
    own_products(d, st, p)
    arrive(corner_copies)
    corner_edges(cin, st, et)
    arrive(row_copies)
    edge_products(d, st, et, p)
    gram_fields(st, f8)
    weigh(f8, u, w)
    spread(w, wc, we)
    edge_mix(p, we)
    best_scores(p, inv, wc, o_ref)
    everything = [exchange] + y_first + y_second + mid_first + mid_second + last_first + last_second + final
    for copy in everything + row_copies + edge_copies + corner_copies:
        copy.wait_send()


def on_device(patterns, scan_mask, neighbour_mask, dictionary):
    k1, k2, eye, order_t = tables()
    vmem = pl.BlockSpec(memory_space=pltpu.VMEM)
    bf, f32 = jnp.bfloat16, jnp.float32
    return pl.pallas_call(
        index_kernel,
        in_specs=[pl.BlockSpec(memory_space=pl.ANY)] + [vmem] * 7,
        out_specs=vmem,
        out_shape=jax.ShapeDtypeStruct((2, TOP, ROWS_DEV, COLS_DEV), f32),
        scratch_shapes=[
            pltpu.VMEM((2, RUN, ROWS_DEV, COLS_DEV), bf),
            pltpu.VMEM((RUN * 8, 128), f32),
            pltpu.VMEM((4, GROUPS, RUN, 256), bf),
            pltpu.VMEM((4, GROUPS, GROUPS, 16, 256), f32),
            pltpu.VMEM((4, 4, 64, DEPTH), bf),
            pltpu.VMEM((8, DEPTH), f32),
            pltpu.VMEM((8, DEPTH), f32),
            pltpu.VMEM((HELD, DEPTH), bf),
            pltpu.VMEM((2, 16, DEPTH), bf),
            pltpu.VMEM((2, 16, DEPTH), bf),
            pltpu.VMEM((2, 16, DEPTH), bf),
            pltpu.VMEM((2, 16, DEPTH), bf),
            pltpu.VMEM((32, DEPTH), f32),
            pltpu.VMEM((11, 1024, 128), f32),
            pltpu.VMEM((9, 8, LANES), f32),
            pltpu.VMEM((8, LANES), f32),
            pltpu.VMEM((16, LANES), f32),
            pltpu.VMEM((8, 16, 128), f32),
            pltpu.VMEM((8, 128), f32),
            pltpu.VMEM((1024, 128), f32),
            pltpu.SemaphoreType.DMA((2,)),
            pltpu.SemaphoreType.DMA((2, COPIES)),
        ],
        compiler_params=pltpu.CompilerParams(
            vmem_limit_bytes=67_043_328, collective_id=0, has_side_effects=True
        ),
        name="index",
    )(patterns, k1, k2, eye, order_t, scan_mask, neighbour_mask, dictionary)


def solution(mesh):
    in_specs = (
        P(None, "strip", "dict"),
        P("strip", "dict"),
        P(None, "strip", "dict"),
        P(None, ("strip", "dict"), None),
    )
    out_specs = P(None, None, "strip", "dict")
    return jax.shard_map(
        on_device, mesh=mesh, in_specs=in_specs, out_specs=out_specs, check_vma=False
    )
```

```python
import functools

import jax
import jax.numpy as jnp
import numpy as np
from jax import lax
from jax.experimental import pallas as pl
from jax.experimental.pallas import tpu as pltpu
from jax.sharding import PartitionSpec as P

PH = 60
NPIX = PH * PH
TOP = 4
epsilon = 1e-05
nlpar_scale = 2.0

GROUPS = 15
RUN = 240
RUN_PAD = 256
DEPTH = GROUPS * RUN_PAD
PITCH = 160
LEAD = 336
COLS_DEV = 128
ROWS_DEV = 8
TILES = 7
LANES = TILES * 256
HELD = LEAD + LANES
OFFSETS = tuple(PITCH * a + b for a in (-1, 0, 1) for b in (-1, 0, 1))
NT = (((1,), (1,)), ((), ()))


def tables():
    positions = np.arange(PH, dtype=np.float64)
    spread_px = PH / 8.0
    profile = np.exp(-((positions[:, None] - positions[None, :]) ** 2) / (2.0 * spread_px**2))
    k = profile / profile.sum(axis=1, keepdims=True)
    q = np.arange(RUN)
    d, low = (q // 16) * 4 + (q // 4) % 4, q % 4
    src_a, src_b = q // PH, q % PH
    same = low[:, None] == src_a[None, :]
    first = np.where(same, k[d[:, None], src_b[None, :]], 0.0)
    order = np.where(same & (d[:, None] == src_b[None, :]), 1.0, 0.0)
    e = (q // 16) * 4 + low
    d4 = (q // 4) % 4
    second = np.where(d4[:, None] == d4[None, :], k[e[:, None], e[None, :]], 0.0)
    bf = functools.partial(jnp.asarray, dtype=jnp.bfloat16)
    order_t = np.zeros((RUN, RUN_PAD))
    order_t[:, :RUN] = order.T
    return bf(np.concatenate([first, order])), bf(second), bf(np.eye(256)), bf(order_t)


def prepare(d_ref, order_ref, own):
    x = jnp.concatenate([d_ref[0].astype(jnp.float32), d_ref[1].astype(jnp.float32)], axis=0)
    inv = 1.0 / jnp.sqrt(jnp.sum(x * x, axis=1, keepdims=True) / NPIX + epsilon)
    hi = inv.astype(jnp.bfloat16).astype(jnp.float32)
    mid = (inv - hi).astype(jnp.bfloat16).astype(jnp.float32)
    low = inv - hi - mid
    xb = x.astype(jnp.bfloat16)
    for ge in range(GROUPS):
        run = xb[:, ge * RUN : (ge + 1) * RUN]
        out = jnp.dot(run, order_ref[...], preferred_element_type=jnp.float32)
        if ge == GROUPS - 1:
            lane = lax.broadcasted_iota(jnp.int32, out.shape, 1)
            for i, piece in enumerate((hi, mid, low)):
                out = jnp.where(lane == RUN + i, piece, out)
        own[:, ge * RUN_PAD : (ge + 1) * RUN_PAD] = out


def first_pass(g, x_ref, k1_ref, xs, h, c):
    for j in range(6):
        part = x_ref[pl.ds(j * 40, 40)].astype(jnp.float32)
        xs[pl.ds(j * 320, 320), :] = part.reshape(320, 128)
    h_at = pl.ds(pl.multiple_of(g * 16, 16), 16)
    for n in range(4):
        even = xs[pl.ds(2 * n, RUN, stride=8), :].astype(jnp.bfloat16)
        odd = xs[pl.ds(2 * n + 1, RUN, stride=8), :].astype(jnp.bfloat16)
        pair = jnp.concatenate([even, odd], axis=1)
        out = jnp.dot(k1_ref[...], pair, preferred_element_type=jnp.float32)
        h[n, :, h_at, :] = out[:RUN].astype(jnp.bfloat16).reshape(GROUPS, 16, 256)
        c[n, g] = out[RUN:].reshape(GROUPS, 16, 256)


def second_pass(n, k2_ref, eye_ref, m_ref, h, c, st):
    def second(dc, carry):
        total, square = carry
        out = jnp.dot(k2_ref[...], h[n, dc], preferred_element_type=jnp.float32)
        corrected = c[n, :, dc] - out.reshape(GROUPS, 16, 256)
        c[n, :, dc] = corrected
        part = corrected.reshape(2 * GROUPS, 8, 256)
        return total + jnp.sum(part, axis=0), square + jnp.sum(part * part, axis=0)

    zero = jnp.zeros((8, 256), jnp.float32)
    total, square = lax.fori_loop(0, GROUPS, second, (zero, zero), unroll=15)
    mean = jnp.sum(total, axis=0, keepdims=True) / NPIX
    var = jnp.sum(square, axis=0, keepdims=True) / NPIX - mean * mean
    mask = jnp.concatenate([m_ref[2 * n : 2 * n + 1, :], m_ref[2 * n + 1 : 2 * n + 2, :]], axis=1)
    scale = mask.astype(jnp.float32) / jnp.sqrt(jnp.maximum(var, 0.0) + epsilon)
    shift = mean * scale

    def third(ge, carry):
        v = (c[n, ge].reshape(RUN, 256) * scale - shift).astype(jnp.bfloat16)
        v = jnp.concatenate([v, jnp.zeros((16, 256), jnp.bfloat16)], axis=0)
        out = lax.dot_general(eye_ref[...], v, NT, preferred_element_type=jnp.float32)
        out = out.astype(jnp.bfloat16)
        at = pl.ds(pl.multiple_of(ge * RUN_PAD, RUN_PAD), RUN_PAD)
        st[pl.ds(own_start(2 * n), 128), at] = out[:128]
        st[pl.ds(own_start(2 * n + 1), 128), at] = out[128:]
        return carry

    lax.fori_loop(0, GROUPS, third, 0, unroll=15)


def row_start(scan_row):
    return LEAD + PITCH * scan_row


def own_start(r):
    return row_start(r + 1) + 16


def gram_fields(st, f8, begin, end, tile_of):
    row_at = lax.broadcasted_iota(jnp.int32, (136, 128), 0)
    lane_at = lax.broadcasted_iota(jnp.int32, (136, 128), 1)
    slots = {}
    for kk in range(9):
        for low in range(min(kk + 1, 8)):
            slots.setdefault(OFFSETS[kk] - OFFSETS[low], []).append((kk, low))

    def tile(i, carry):
        n0 = pl.multiple_of(tile_of(i) * 256, 256)
        rows = st[pl.ds(n0, LEAD + 256), :]
        cols = st[pl.ds(pl.multiple_of(n0 + LEAD, 16), 256), :]
        g = lax.dot_general(rows, cols, NT, preferred_element_type=jnp.float32)
        for half in range(2):
            lanes = g[:, half * 128 : (half + 1) * 128]
            for o, where_to in slots.items():
                first = LEAD + half * 128 - o
                start = min(first // 8 * 8, LEAD + 256 - 136)
                hit = row_at + (start - first) == lane_at
                value = jnp.sum(jnp.where(hit, lanes[start : start + 136], 0.0), axis=0, keepdims=True)
                at = pl.ds(pl.multiple_of(n0 + half * 128, 128), 128)
                for kk, low in where_to:
                    f8[kk, low : low + 1, at] = value
        return carry

    lax.fori_loop(begin, end, tile, 0)


def usable_rows(nm_ref, u, first_row, first_col, all_rows, all_cols):
    u[...] = jnp.zeros_like(u)
    kk = lax.broadcasted_iota(jnp.int32, (8, 128), 0)
    kk = kk + (kk >= 4).astype(jnp.int32)
    down = (kk >= 3).astype(jnp.int32) + (kk >= 6).astype(jnp.int32) - 1
    right = kk - 3 * (down + 1) - 1
    col = lax.broadcasted_iota(jnp.int32, (8, 128), 1) + first_col + right
    col_ok = (col >= 0) & (col < all_cols)
    for r in range(ROWS_DEV):
        row = down + (first_row + r)
        ok = (row >= 0) & (row < all_rows) & col_ok & (nm_ref[:, r, :] == 1)
        at = PITCH * (r + 1) + 16
        u[:, at : at + 128] = ok.astype(jnp.float32)


def weigh(f8, u, w):
    def turn(x, off):
        return x if off == 0 else pltpu.roll(x, (-off) % LANES, 1)

    n = f8[0, 0:1, :]
    centre = f8[4]
    placed = {4: centre}
    for kk in (0, 1, 2, 3, 5, 6, 7, 8):
        placed[kk] = turn(f8[kk], OFFSETS[kk])
    last = turn(jnp.broadcast_to(n, (8, LANES)), OFFSETS[8])[0:1]
    own = [placed[kk][kk : kk + 1] if kk < 8 else last for kk in range(9)]
    den = jnp.ones((1, LANES), jnp.float32)
    weights = []
    for kk in range(9):
        if kk == 4:
            value = jnp.ones((1, LANES), jnp.float32)
        else:
            dot = centre[kk : kk + 1] if kk < 4 else placed[kk][4:5]
            distance = (n + own[kk] - 2.0 * dot) / NPIX
            slot = kk if kk < 4 else kk - 1
            value = jnp.where(u[slot : slot + 1, :] > 0.5, jnp.exp(-distance / nlpar_scale), 0.0)
            den = den + value
        weights.append(value)
        w[kk : kk + 1, :] = value
    lows = w[0:8, :]
    quad = jnp.zeros((1, LANES), jnp.float32)
    for kk in range(9):
        part = 2.0 * jnp.sum(lows * placed[kk], axis=0, keepdims=True)
        self_term = weights[kk] * own[kk]
        part = part - self_term if kk < 8 else part + self_term
        quad = quad + weights[kk] * part
    square = jnp.maximum(quad, 0.0) / (den * den) / NPIX
    w[9:10, :] = 1.0 / (jnp.sqrt(square + epsilon) * den * NPIX)


def spread(w, wc, we):
    lane = lax.broadcasted_iota(jnp.int32, (16, 128), 1)
    edge = jnp.zeros((16, 128), jnp.float32)
    kinds = lax.broadcasted_iota(jnp.int32, (16, 128), 0)
    left = (kinds == 0) | (kinds == 3) | (kinds == 6)
    right = (kinds == 2) | (kinds == 5) | (kinds == 8)
    for r in range(ROWS_DEV):
        at = PITCH * (r + 1) + 16
        here = w[:, at : at + 128]
        before = w[:, at + 1 : at + 129]
        after = w[:, at - 1 : at + 127]
        wc[r] = jnp.where(left, before, jnp.where(right, after, here))
        R = r + 1
        edge = jnp.where(lane == 2 * R, pltpu.roll(here, 2 * R, 1), edge)
        edge = jnp.where(lane == 2 * R + 1, pltpu.roll(here, 2 * R + 2, 1), edge)
    odd = lane[0:1] % 2 == 1
    for i in range(3):
        we[i : i + 1, :] = jnp.where(odd, edge[3 * i + 2 : 3 * i + 3], edge[3 * i : 3 * i + 1])


def own_edges(st, et, eout):
    for r in range(ROWS_DEV):
        top = own_start(r)
        et[r : r + 1, :] = st[pl.ds(top, 16), :].astype(jnp.float32)[0:1]
        et[16 + r : 17 + r, :] = st[pl.ds(top + 112, 16), :].astype(jnp.float32)[15:16]
    et[8:16, :] = jnp.zeros((8, DEPTH), jnp.float32)
    et[24:32, :] = jnp.zeros((8, DEPTH), jnp.float32)
    eout[0] = et[0:16, :].astype(jnp.bfloat16)
    eout[1] = et[16:32, :].astype(jnp.bfloat16)


def place_edges(R, left, right, st, et):
    et[2 * R : 2 * R + 1, :] = left
    et[2 * R + 1 : 2 * R + 2, :] = right
    st[pl.ds(row_start(R), 16), :] = jnp.broadcast_to(left, (16, DEPTH)).astype(jnp.bfloat16)
    st[pl.ds(row_start(R) + 144, 16), :] = jnp.broadcast_to(right, (16, DEPTH)).astype(jnp.bfloat16)


def inner_edges(ein, st, et, cout):
    left, right = ein[0].astype(jnp.float32), ein[1].astype(jnp.float32)
    row = lax.broadcasted_iota(jnp.int32, (16, DEPTH), 0)
    for i, r in enumerate((0, ROWS_DEV - 1)):
        both = jnp.where(row == 0, left[r : r + 1], right[r : r + 1])
        cout[i] = both.astype(jnp.bfloat16)
    for r in range(ROWS_DEV):
        place_edges(r + 1, left[r : r + 1], right[r : r + 1], st, et)


def corner_edges(cin, st, et):
    for i, R in enumerate((0, ROWS_DEV + 1)):
        both = cin[i].astype(jnp.float32)
        place_edges(R, both[0:1], both[1:2], st, et)
    et[20:32, :] = jnp.zeros((12, DEPTH), jnp.float32)


def pair_product(d, st, p, i, j):
    a = pl.multiple_of(LEAD + 16 + PITCH * i, 16)
    b = pl.multiple_of(LEAD + 16 + PITCH * j, 16)
    rows = jnp.concatenate([st[pl.ds(a, 128), :], st[pl.ds(b, 128), :]], axis=0)
    out = lax.dot_general(d[...].reshape(1024, DEPTH), rows, NT, preferred_element_type=jnp.float32)
    p[i] = out[:, :128]
    p[j] = out[:, 128:]


def own_products(d, st, p):
    def pair(i, carry):
        pair_product(d, st, p, 2 * i + 1, 2 * i + 2)
        return carry

    lax.fori_loop(0, ROWS_DEV // 2, pair, 0)


def edge_products(d, st, et, p):
    pair_product(d, st, p, 0, ROWS_DEV + 1)
    edge = et[...].astype(jnp.bfloat16)
    edge = jnp.concatenate([edge, jnp.zeros((96, DEPTH), jnp.bfloat16)], axis=0)
    p[10] = lax.dot_general(d[...].reshape(1024, DEPTH), edge, NT, preferred_element_type=jnp.float32)


def entry_norms(d, inv):
    tail = d[:, :, :, DEPTH - 128 :].reshape(1024, 128).astype(jnp.float32)
    at = RUN - 128
    value = tail[:, at : at + 1] + tail[:, at + 1 : at + 2] + tail[:, at + 2 : at + 3]
    inv[...] = jnp.broadcast_to(value, inv.shape)


def edge_mix(p, we):
    def step(k, carry):
        at = pl.ds(pl.multiple_of(k * 8, 8), 8)
        e = p[10, at, :]
        mix = e * we[1:2, :] + pltpu.roll(e, 2, 1) * we[0:1, :] + pltpu.roll(e, 126, 1) * we[2:3, :]
        p[10, at, :] = mix
        return carry

    lax.fori_loop(0, 128, step, 0, unroll=8)


def order(x, i, j):
    x[i], x[j] = jnp.maximum(x[i], x[j]), jnp.minimum(x[i], x[j])


def merge_best(best, other):
    m = [jnp.maximum(best[i], other[3 - i]) for i in range(4)]
    for i, j in ((0, 2), (1, 3), (0, 1), (2, 3)):
        order(m, i, j)
    return m


STEP = 32


def best_scores(p, inv, wc, o_ref):
    lane = lax.broadcasted_iota(jnp.int32, (8, 128), 1)
    first, last = lane == 0, lane == 127

    def scan_row(r, carry):
        wt = [jnp.broadcast_to(wc[r, kk : kk + 1, :], (8, 128)) for kk in range(9)]
        turn = 125 - 2 * r

        def score(at):
            up, mid, down = p[r, at, :], p[r + 1, at, :], p[r + 2, at, :]
            edge = pltpu.roll(p[10, at, :], turn, 1)
            left = up * wt[0] + mid * wt[3] + down * wt[6]
            right = up * wt[2] + mid * wt[5] + down * wt[8]
            here = up * wt[1] + mid + down * wt[7]
            left = jnp.where(last, edge, left)
            right = jnp.where(first, edge, right)
            return (here + pltpu.roll(left, 1, 1) + pltpu.roll(right, 127, 1)) * inv[at, :]

        def step(k, best):
            best = list(best)
            for i in range(0, STEP, 4):
                v = [score(pl.ds(pl.multiple_of(k * (8 * STEP) + (i + j) * 8, 8), 8)) for j in range(4)]
                for a, b in ((0, 1), (2, 3), (0, 2), (1, 3), (1, 2)):
                    order(v, a, b)
                best = merge_best(best, v)
            return tuple(best)

        low = jnp.full((8, 128), -jnp.inf, jnp.float32)
        best = lax.fori_loop(0, 128 // STEP, step, (low, low, low, low))
        for shift in (6, 7):
            best = merge_best(best, [pltpu.roll(b, shift, 0) for b in best])
        scale = wc[r, 9:10, :]
        for j in range(TOP):
            o_ref[0, j, pl.ds(r, 1), :] = best[j][0:1] * scale
            o_ref[1, j, pl.ds(r, 1), :] = best[j][4:5] * scale
        return carry

    lax.fori_loop(0, ROWS_DEV, scan_row, 0)


def send(src, dst, sems, i, device):
    return pltpu.make_async_remote_copy(
        src_ref=src,
        dst_ref=dst,
        send_sem=sems.at[0, i],
        recv_sem=sems.at[1, i],
        device_id=device,
        device_id_type=pl.DeviceIdType.MESH,
    )


COPIES = 48
BATCH = 3


def index_kernel(x_hbm, k1_ref, k2_ref, eye_ref, order_ref, m_ref, nm_ref, dict_ref, o_ref,
                 xbuf, xs, h, c, d, own, sib, st, eout, ein, cout, cin,
                 et, p, f8, u, w, wc, we, inv, xsem, sems):
    strip, slot = lax.axis_index("strip"), lax.axis_index("dict")
    core, zl = slot % 2, slot // 2
    zh, ix, iy = strip // 16, (strip // 4) % 4, strip % 4
    iz = zh * 2 + zl

    def chip(x, y, z):
        x, y, z = x % 4, y % 4, z % 4
        return ((z // 2) * 16 + x * 4 + y, (z % 2) * 2 + core)

    sibling = (strip, zl * 2 + (1 - core))
    x_up, x_down = chip(ix + 1, iy, iz), chip(ix + 3, iy, iz)
    y_up, y_down = chip(ix, iy + 1, iz), chip(ix, iy + 3, iz)
    z_up, z_down = chip(ix, iy, iz + 1), chip(ix, iy, iz + 3)
    row_up, row_down = ((strip + 31) % 32, slot), ((strip + 1) % 32, slot)
    col_left, col_right = (strip, (slot + 3) % 4), (strip, (slot + 1) % 4)

    def fetch(g, at):
        rows = pl.ds(pl.multiple_of(g * (BATCH * RUN), BATCH * RUN), BATCH * RUN)
        return pltpu.make_async_copy(x_hbm.at[rows], xbuf.at[at], xsem.at[at])

    fetch(0, 0).start()
    peers = (sibling, x_up, x_down, y_up, y_down, z_up, z_down, row_up, row_down, col_left, col_right)
    barrier = pltpu.get_barrier_semaphore()
    for peer in peers:
        pl.semaphore_signal(barrier, inc=1, device_id=peer, device_id_type=pl.DeviceIdType.MESH)
    prepare(dict_ref, order_ref, own)
    pl.semaphore_wait(barrier, len(peers))
    exchange = send(own, sib, sems, 0, sibling)
    exchange.start()

    base = pl.multiple_of(core * 1920, 128)
    half = pl.ds(base, 1920)
    part_a = pl.ds(base, 1024)
    part_b = pl.ds(pl.multiple_of(base + 1024, 128), 896)
    xu, xd, yu, yd, zu, zd = [(v % 4) for v in (ix + 1, ix + 3, iy + 1, iy + 3, iz + 1, iz + 3)]

    def same(ref, i, device):
        return send(ref, ref, sems, i, device)

    def rows_of(y):
        return pl.ds(pl.multiple_of(y * 16, 16), 16)

    upper, lower = pl.ds(0, 32), pl.ds(32, 32)
    y_first = [same(d.at[ix, iz, rows_of(iy), half], 1, y_up), same(d.at[ix, iz, rows_of(iy), half], 2, y_down)]
    y_second = [same(d.at[ix, iz, rows_of(yd), part_a], 3, y_up), same(d.at[ix, iz, rows_of(yu), part_b], 4, y_down)]
    mid_first = [
        same(d.at[ix, iz, :, part_a], 5, z_up),
        same(d.at[ix, iz, :, part_a], 6, z_down),
        same(d.at[ix, iz, :, part_b], 7, x_up),
        same(d.at[ix, iz, :, part_b], 8, x_down),
    ]
    mid_second = [
        same(d.at[ix, zd, upper, part_a], 9, z_up),
        same(d.at[ix, zu, lower, part_a], 10, z_down),
        same(d.at[xd, iz, upper, part_b], 11, x_up),
        same(d.at[xu, iz, lower, part_b], 12, x_down),
    ]
    last_first = [
        same(d.at[ix, :, :, part_a], 13, x_up),
        same(d.at[ix, :, :, part_a], 14, x_down),
        same(d.at[:, iz, :, part_b], 15, z_up),
        same(d.at[:, iz, :, part_b], 16, z_down),
        same(d.at[ix, :, :, part_a], 17, sibling),
        same(d.at[:, iz, :, part_b], 18, sibling),
    ]
    first_two, last_two = pl.ds(0, 2), pl.ds(2, 2)
    last_second = [
        same(d.at[xd, first_two, :, part_a], 19, x_up),
        same(d.at[xu, last_two, :, part_a], 20, x_down),
        same(d.at[first_two, zd, :, part_b], 21, z_up),
        same(d.at[last_two, zu, :, part_b], 22, z_down),
        same(d.at[xd, :, :, part_a], 23, sibling),
        same(d.at[xu, :, :, part_a], 24, sibling),
        same(d.at[:, zd, :, part_b], 25, sibling),
        same(d.at[:, zu, :, part_b], 26, sibling),
    ]
    xo, zo = (ix + 2) % 4, (iz + 2) % 4
    final = [
        same(d.at[xo, :, :, part_a], 27, sibling),
        same(d.at[:, zo, :, part_b], 28, sibling),
    ]

    def start(copies):
        for copy in copies:
            copy.start()

    def arrive(copies):
        for copy in copies:
            copy.wait_recv()

    def begin():
        exchange.wait_recv()
        mine, other = own[:, half], sib[:, half]
        first = core == 0
        both = jnp.concatenate([jnp.where(first, mine, other), jnp.where(first, other, mine)], axis=0)
        d[ix, iz, rows_of(iy), half] = both.astype(jnp.bfloat16)
        start(y_first)

    def forward(arrived, following):
        def act():
            arrive(arrived)
            start(following)
        return act

    events = {
        0: begin,
        1: forward(y_first, y_second),
        2: forward(y_second, mid_first),
        4: forward(mid_first, mid_second),
    }
    st[pl.ds(0, LEAD), :] = jnp.zeros((LEAD, DEPTH), jnp.bfloat16)
    tail = LANES - 10 * PITCH
    st[pl.ds(LEAD + 10 * PITCH, tail), :] = jnp.zeros((tail, DEPTH), jnp.bfloat16)
    w[...] = jnp.zeros_like(w)
    f8[...] = jnp.zeros_like(f8)
    usable_rows(nm_ref, u, strip * ROWS_DEV, slot * COLS_DEV, 32 * ROWS_DEV, 4 * COLS_DEV)

    def chunk(g, carry):
        at = g % 2

        @pl.when(g + 1 < GROUPS // BATCH)
        def _():
            fetch(g + 1, 1 - at).start()

        fetch(g, at).wait()
        for i in range(BATCH):
            first_pass(g * BATCH + i, xbuf.at[at, pl.ds(i * RUN, RUN)], k1_ref, xs.at[i], h, c)
        for when, act in events.items():
            pl.when(g == when)(act)
        return carry

    lax.fori_loop(0, GROUPS // BATCH, chunk, 0)

    row_copies = [
        send(st.at[pl.ds(own_start(7), 128), :], st.at[pl.ds(own_start(-1), 128), :], sems, 29, row_down),
        send(st.at[pl.ds(own_start(0), 128), :], st.at[pl.ds(own_start(8), 128), :], sems, 30, row_up),
    ]
    edge_copies = [
        send(eout.at[0], ein.at[1], sems, 31, col_left),
        send(eout.at[1], ein.at[0], sems, 32, col_right),
    ]
    corner_copies = [
        send(cout.at[0], cin.at[1], sems, 33, row_up),
        send(cout.at[1], cin.at[0], sems, 34, row_down),
    ]
    second_pass(3, k2_ref, eye_ref, m_ref, h, c, st)
    row_copies[0].start()
    second_pass(0, k2_ref, eye_ref, m_ref, h, c, st)
    row_copies[1].start()
    forward(mid_second, last_first)()
    second_pass(1, k2_ref, eye_ref, m_ref, h, c, st)
    second_pass(2, k2_ref, eye_ref, m_ref, h, c, st)
    own_edges(st, et, eout)
    start(edge_copies)
    arrive(edge_copies)
    inner_edges(ein, st, et, cout)
    start(corner_copies)
    gram_fields(st, f8, 2, 5, lambda i: i)
    forward(last_first, last_second)()
    arrive(corner_copies)
    corner_edges(cin, st, et)
    forward(last_second, final)()
    arrive(row_copies)
    gram_fields(st, f8, 0, 4, lambda i: i + 3 * (i // 2))
    weigh(f8, u, w)
    spread(w, wc, we)
    arrive(final)
    entry_norms(d, inv)
    own_products(d, st, p)
    edge_products(d, st, et, p)
    edge_mix(p, we)
    best_scores(p, inv, wc, o_ref)
    everything = [exchange] + y_first + y_second + mid_first + mid_second + last_first + last_second + final
    for copy in everything + row_copies + edge_copies + corner_copies:
        copy.wait_send()


def on_device(patterns, scan_mask, neighbour_mask, dictionary):
    k1, k2, eye, order_t = tables()
    vmem = pl.BlockSpec(memory_space=pltpu.VMEM)
    bf, f32 = jnp.bfloat16, jnp.float32
    return pl.pallas_call(
        index_kernel,
        in_specs=[pl.BlockSpec(memory_space=pl.ANY)] + [vmem] * 7,
        out_specs=vmem,
        out_shape=jax.ShapeDtypeStruct((2, TOP, ROWS_DEV, COLS_DEV), f32),
        scratch_shapes=[
            pltpu.VMEM((2, BATCH * RUN, ROWS_DEV, COLS_DEV), bf),
            pltpu.VMEM((BATCH, RUN * 8, 128), f32),
            pltpu.VMEM((4, GROUPS, RUN, 256), bf),
            pltpu.VMEM((4, GROUPS, GROUPS, 16, 256), f32),
            pltpu.VMEM((4, 4, 64, DEPTH), bf),
            pltpu.VMEM((8, DEPTH), f32),
            pltpu.VMEM((8, DEPTH), f32),
            pltpu.VMEM((HELD, DEPTH), bf),
            pltpu.VMEM((2, 16, DEPTH), bf),
            pltpu.VMEM((2, 16, DEPTH), bf),
            pltpu.VMEM((2, 16, DEPTH), bf),
            pltpu.VMEM((2, 16, DEPTH), bf),
            pltpu.VMEM((32, DEPTH), f32),
            pltpu.VMEM((11, 1024, 128), f32),
            pltpu.VMEM((9, 8, LANES), f32),
            pltpu.VMEM((8, LANES), f32),
            pltpu.VMEM((16, LANES), f32),
            pltpu.VMEM((8, 16, 128), f32),
            pltpu.VMEM((8, 128), f32),
            pltpu.VMEM((1024, 128), f32),
            pltpu.SemaphoreType.DMA((2,)),
            pltpu.SemaphoreType.DMA((2, COPIES)),
        ],
        compiler_params=pltpu.CompilerParams(
            vmem_limit_bytes=67_043_328, collective_id=0, has_side_effects=True
        ),
        name="index",
    )(patterns, k1, k2, eye, order_t, scan_mask, neighbour_mask, dictionary)


def solution(mesh):
    in_specs = (
        P(None, "strip", "dict"),
        P("strip", "dict"),
        P(None, "strip", "dict"),
        P(None, ("strip", "dict"), None),
    )
    out_specs = P(None, None, "strip", "dict")
    return jax.shard_map(
        on_device, mesh=mesh, in_specs=in_specs, out_specs=out_specs, check_vma=False
    )
```

```python
import functools

import jax
import jax.numpy as jnp
import numpy as np
from jax import lax
from jax.experimental import pallas as pl
from jax.experimental.pallas import tpu as pltpu
from jax.sharding import PartitionSpec as P

PH = 60
NPIX = PH * PH
TOP = 4
epsilon = 1e-05
nlpar_scale = 2.0

GROUPS = 15
RUN = 240
RUN_PAD = 256
DEPTH = GROUPS * RUN_PAD
PITCH = 160
LEAD = 336
COLS_DEV = 128
ROWS_DEV = 8
TILES = 7
LANES = TILES * 256
HELD = LEAD + LANES
OFFSETS = tuple(PITCH * a + b for a in (-1, 0, 1) for b in (-1, 0, 1))
NT = (((1,), (1,)), ((), ()))


def tables():
    positions = np.arange(PH, dtype=np.float64)
    spread_px = PH / 8.0
    profile = np.exp(-((positions[:, None] - positions[None, :]) ** 2) / (2.0 * spread_px**2))
    k = profile / profile.sum(axis=1, keepdims=True)
    q = np.arange(RUN)
    d, low = (q // 16) * 4 + (q // 4) % 4, q % 4
    src_a, src_b = q // PH, q % PH
    same = low[:, None] == src_a[None, :]
    first = np.where(same, k[d[:, None], src_b[None, :]], 0.0)
    order = np.where(same & (d[:, None] == src_b[None, :]), 1.0, 0.0)
    e = (q // 16) * 4 + low
    d4 = (q // 4) % 4
    second = np.where(d4[:, None] == d4[None, :], k[e[:, None], e[None, :]], 0.0)
    bf = functools.partial(jnp.asarray, dtype=jnp.bfloat16)
    order_t = np.zeros((RUN, RUN_PAD))
    order_t[:, :RUN] = order.T
    return bf(np.concatenate([first, order])), bf(second), bf(np.eye(256)), bf(order_t)


def prepare(d_ref, order_ref, own):
    x = jnp.concatenate([d_ref[0].astype(jnp.float32), d_ref[1].astype(jnp.float32)], axis=0)
    inv = 1.0 / jnp.sqrt(jnp.sum(x * x, axis=1, keepdims=True) / NPIX + epsilon)
    hi = inv.astype(jnp.bfloat16).astype(jnp.float32)
    mid = (inv - hi).astype(jnp.bfloat16).astype(jnp.float32)
    low = inv - hi - mid
    xb = x.astype(jnp.bfloat16)
    for ge in range(GROUPS):
        run = xb[:, ge * RUN : (ge + 1) * RUN]
        out = jnp.dot(run, order_ref[...], preferred_element_type=jnp.float32)
        if ge == GROUPS - 1:
            lane = lax.broadcasted_iota(jnp.int32, out.shape, 1)
            for i, piece in enumerate((hi, mid, low)):
                out = jnp.where(lane == RUN + i, piece, out)
        own[:, ge * RUN_PAD : (ge + 1) * RUN_PAD] = out


def first_pass(g, x_ref, k1_ref, xs, h, c):
    for j in range(6):
        part = x_ref[pl.ds(j * 40, 40)].astype(jnp.float32)
        xs[pl.ds(j * 320, 320), :] = part.reshape(320, 128)
    h_at = pl.ds(pl.multiple_of(g * 16, 16), 16)
    for n in range(4):
        even = xs[pl.ds(2 * n, RUN, stride=8), :].astype(jnp.bfloat16)
        odd = xs[pl.ds(2 * n + 1, RUN, stride=8), :].astype(jnp.bfloat16)
        pair = jnp.concatenate([even, odd], axis=1)
        out = jnp.dot(k1_ref[...], pair, preferred_element_type=jnp.float32)
        h[n, :, h_at, :] = out[:RUN].astype(jnp.bfloat16).reshape(GROUPS, 16, 256)
        c[n, g] = out[RUN:].reshape(GROUPS, 16, 256)


def second_pass(n, k2_ref, eye_ref, m_ref, h, c, st):
    def second(dc, carry):
        total, square = carry
        out = jnp.dot(k2_ref[...], h[n, dc], preferred_element_type=jnp.float32)
        corrected = c[n, :, dc] - out.reshape(GROUPS, 16, 256)
        c[n, :, dc] = corrected
        part = corrected.reshape(2 * GROUPS, 8, 256)
        return total + jnp.sum(part, axis=0), square + jnp.sum(part * part, axis=0)

    zero = jnp.zeros((8, 256), jnp.float32)
    total, square = lax.fori_loop(0, GROUPS, second, (zero, zero), unroll=15)
    mean = jnp.sum(total, axis=0, keepdims=True) / NPIX
    var = jnp.sum(square, axis=0, keepdims=True) / NPIX - mean * mean
    mask = jnp.concatenate([m_ref[2 * n : 2 * n + 1, :], m_ref[2 * n + 1 : 2 * n + 2, :]], axis=1)
    scale = mask.astype(jnp.float32) / jnp.sqrt(jnp.maximum(var, 0.0) + epsilon)
    shift = mean * scale

    def third(ge, carry):
        v = (c[n, ge].reshape(RUN, 256) * scale - shift).astype(jnp.bfloat16)
        v = jnp.concatenate([v, jnp.zeros((16, 256), jnp.bfloat16)], axis=0)
        out = lax.dot_general(eye_ref[...], v, NT, preferred_element_type=jnp.float32)
        out = out.astype(jnp.bfloat16)
        at = pl.ds(pl.multiple_of(ge * RUN_PAD, RUN_PAD), RUN_PAD)
        st[pl.ds(own_start(2 * n), 128), at] = out[:128]
        st[pl.ds(own_start(2 * n + 1), 128), at] = out[128:]
        return carry

    lax.fori_loop(0, GROUPS, third, 0, unroll=15)


def row_start(scan_row):
    return LEAD + PITCH * scan_row


def own_start(r):
    return row_start(r + 1) + 16


def gram_fields(st, f8, begin, end, tile_of):
    row_at = lax.broadcasted_iota(jnp.int32, (136, 128), 0)
    lane_at = lax.broadcasted_iota(jnp.int32, (136, 128), 1)
    slots = {}
    for kk in range(9):
        for low in range(min(kk + 1, 8)):
            slots.setdefault(OFFSETS[kk] - OFFSETS[low], []).append((kk, low))

    def tile(i, carry):
        n0 = pl.multiple_of(tile_of(i) * 256, 256)
        rows = st[pl.ds(n0, LEAD + 256), :]
        cols = st[pl.ds(pl.multiple_of(n0 + LEAD, 16), 256), :]
        g = lax.dot_general(rows, cols, NT, preferred_element_type=jnp.float32)
        for half in range(2):
            lanes = g[:, half * 128 : (half + 1) * 128]
            for o, where_to in slots.items():
                first = LEAD + half * 128 - o
                start = min(first // 8 * 8, LEAD + 256 - 136)
                hit = row_at + (start - first) == lane_at
                value = jnp.sum(jnp.where(hit, lanes[start : start + 136], 0.0), axis=0, keepdims=True)
                at = pl.ds(pl.multiple_of(n0 + half * 128, 128), 128)
                for kk, low in where_to:
                    f8[kk, low : low + 1, at] = value
        return carry

    lax.fori_loop(begin, end, tile, 0)


def usable_rows(nm_ref, u, first_row, first_col, all_rows, all_cols):
    u[...] = jnp.zeros_like(u)
    kk = lax.broadcasted_iota(jnp.int32, (8, 128), 0)
    kk = kk + (kk >= 4).astype(jnp.int32)
    down = (kk >= 3).astype(jnp.int32) + (kk >= 6).astype(jnp.int32) - 1
    right = kk - 3 * (down + 1) - 1
    col = lax.broadcasted_iota(jnp.int32, (8, 128), 1) + first_col + right
    col_ok = (col >= 0) & (col < all_cols)
    for r in range(ROWS_DEV):
        row = down + (first_row + r)
        ok = (row >= 0) & (row < all_rows) & col_ok & (nm_ref[:, r, :] == 1)
        at = PITCH * (r + 1) + 16
        u[:, at : at + 128] = ok.astype(jnp.float32)


def weigh(f8, u, w):
    def turn(x, off):
        return x if off == 0 else pltpu.roll(x, (-off) % LANES, 1)

    n = f8[0, 0:1, :]
    centre = f8[4]
    placed = {4: centre}
    for kk in (0, 1, 2, 3, 5, 6, 7, 8):
        placed[kk] = turn(f8[kk], OFFSETS[kk])
    last = turn(jnp.broadcast_to(n, (8, LANES)), OFFSETS[8])[0:1]
    own = [placed[kk][kk : kk + 1] if kk < 8 else last for kk in range(9)]
    den = jnp.ones((1, LANES), jnp.float32)
    weights = []
    for kk in range(9):
        if kk == 4:
            value = jnp.ones((1, LANES), jnp.float32)
        else:
            dot = centre[kk : kk + 1] if kk < 4 else placed[kk][4:5]
            distance = (n + own[kk] - 2.0 * dot) / NPIX
            slot = kk if kk < 4 else kk - 1
            value = jnp.where(u[slot : slot + 1, :] > 0.5, jnp.exp(-distance / nlpar_scale), 0.0)
            den = den + value
        weights.append(value)
        w[kk : kk + 1, :] = value
    lows = w[0:8, :]
    quad = jnp.zeros((1, LANES), jnp.float32)
    for kk in range(9):
        part = 2.0 * jnp.sum(lows * placed[kk], axis=0, keepdims=True)
        self_term = weights[kk] * own[kk]
        part = part - self_term if kk < 8 else part + self_term
        quad = quad + weights[kk] * part
    square = jnp.maximum(quad, 0.0) / (den * den) / NPIX
    w[9:10, :] = 1.0 / (jnp.sqrt(square + epsilon) * den * NPIX)


def spread(w, wc, we):
    lane = lax.broadcasted_iota(jnp.int32, (16, 128), 1)
    edge = jnp.zeros((16, 128), jnp.float32)
    kinds = lax.broadcasted_iota(jnp.int32, (16, 128), 0)
    left = (kinds == 0) | (kinds == 3) | (kinds == 6)
    right = (kinds == 2) | (kinds == 5) | (kinds == 8)
    for r in range(ROWS_DEV):
        at = PITCH * (r + 1) + 16
        here = w[:, at : at + 128]
        before = w[:, at + 1 : at + 129]
        after = w[:, at - 1 : at + 127]
        wc[r] = jnp.where(left, before, jnp.where(right, after, here))
        R = r + 1
        edge = jnp.where(lane == 2 * R, pltpu.roll(here, 2 * R, 1), edge)
        edge = jnp.where(lane == 2 * R + 1, pltpu.roll(here, 2 * R + 2, 1), edge)
    odd = lane[0:1] % 2 == 1
    for i in range(3):
        we[i : i + 1, :] = jnp.where(odd, edge[3 * i + 2 : 3 * i + 3], edge[3 * i : 3 * i + 1])


def own_edges(st, et, eout):
    for r in range(ROWS_DEV):
        top = own_start(r)
        et[r : r + 1, :] = st[pl.ds(top, 16), :].astype(jnp.float32)[0:1]
        et[16 + r : 17 + r, :] = st[pl.ds(top + 112, 16), :].astype(jnp.float32)[15:16]
    et[8:16, :] = jnp.zeros((8, DEPTH), jnp.float32)
    et[24:32, :] = jnp.zeros((8, DEPTH), jnp.float32)
    eout[0] = et[0:16, :].astype(jnp.bfloat16)
    eout[1] = et[16:32, :].astype(jnp.bfloat16)


def place_edges(R, left, right, st, et):
    et[2 * R : 2 * R + 1, :] = left
    et[2 * R + 1 : 2 * R + 2, :] = right
    st[pl.ds(row_start(R), 16), :] = jnp.broadcast_to(left, (16, DEPTH)).astype(jnp.bfloat16)
    st[pl.ds(row_start(R) + 144, 16), :] = jnp.broadcast_to(right, (16, DEPTH)).astype(jnp.bfloat16)


def inner_edges(ein, st, et, cout):
    left, right = ein[0].astype(jnp.float32), ein[1].astype(jnp.float32)
    row = lax.broadcasted_iota(jnp.int32, (16, DEPTH), 0)
    for i, r in enumerate((0, ROWS_DEV - 1)):
        both = jnp.where(row == 0, left[r : r + 1], right[r : r + 1])
        cout[i] = both.astype(jnp.bfloat16)
    for r in range(ROWS_DEV):
        place_edges(r + 1, left[r : r + 1], right[r : r + 1], st, et)


def corner_edges(cin, st, et):
    for i, R in enumerate((0, ROWS_DEV + 1)):
        both = cin[i].astype(jnp.float32)
        place_edges(R, both[0:1], both[1:2], st, et)
    et[20:32, :] = jnp.zeros((12, DEPTH), jnp.float32)


def pair_product(d, st, p, i, j):
    a = pl.multiple_of(LEAD + 16 + PITCH * i, 16)
    b = pl.multiple_of(LEAD + 16 + PITCH * j, 16)
    rows = jnp.concatenate([st[pl.ds(a, 128), :], st[pl.ds(b, 128), :]], axis=0)
    out = lax.dot_general(d[...].reshape(1024, DEPTH), rows, NT, preferred_element_type=jnp.float32)
    p[i] = out[:, :128]
    p[j] = out[:, 128:]


def own_products(d, st, p):
    def pair(i, carry):
        pair_product(d, st, p, 2 * i + 1, 2 * i + 2)
        return carry

    lax.fori_loop(0, ROWS_DEV // 2, pair, 0)


def edge_products(d, st, et, p):
    pair_product(d, st, p, 0, ROWS_DEV + 1)
    edge = et[...].astype(jnp.bfloat16)
    edge = jnp.concatenate([edge, jnp.zeros((96, DEPTH), jnp.bfloat16)], axis=0)
    p[10] = lax.dot_general(d[...].reshape(1024, DEPTH), edge, NT, preferred_element_type=jnp.float32)


def entry_norms(d, inv):
    tail = d[:, :, :, :, DEPTH - 128 :].reshape(1024, 128).astype(jnp.float32)
    at = RUN - 128
    value = tail[:, at : at + 1] + tail[:, at + 1 : at + 2] + tail[:, at + 2 : at + 3]
    inv[...] = jnp.broadcast_to(value, inv.shape)


def edge_mix(p, we):
    def step(k, carry):
        at = pl.ds(pl.multiple_of(k * 8, 8), 8)
        e = p[10, at, :]
        mix = e * we[1:2, :] + pltpu.roll(e, 2, 1) * we[0:1, :] + pltpu.roll(e, 126, 1) * we[2:3, :]
        p[10, at, :] = mix
        return carry

    lax.fori_loop(0, 128, step, 0, unroll=16)


def order(x, i, j):
    x[i], x[j] = jnp.maximum(x[i], x[j]), jnp.minimum(x[i], x[j])


def merge_best(best, other):
    m = [jnp.maximum(best[i], other[3 - i]) for i in range(4)]
    for i, j in ((0, 2), (1, 3), (0, 1), (2, 3)):
        order(m, i, j)
    return m


STEP = 32


def best_scores(p, inv, wc, o_ref):
    lane = lax.broadcasted_iota(jnp.int32, (8, 128), 1)
    first, last = lane == 0, lane == 127

    def scan_row(r, carry):
        wt = [jnp.broadcast_to(wc[r, kk : kk + 1, :], (8, 128)) for kk in range(9)]
        turn = 125 - 2 * r

        def score(at):
            up, mid, down = p[r, at, :], p[r + 1, at, :], p[r + 2, at, :]
            edge = pltpu.roll(p[10, at, :], turn, 1)
            left = up * wt[0] + mid * wt[3] + down * wt[6]
            right = up * wt[2] + mid * wt[5] + down * wt[8]
            here = up * wt[1] + mid + down * wt[7]
            left = jnp.where(last, edge, left)
            right = jnp.where(first, edge, right)
            return (here + pltpu.roll(left, 1, 1) + pltpu.roll(right, 127, 1)) * inv[at, :]

        def step(k, best):
            best = list(best)
            for i in range(0, STEP, 4):
                v = [score(pl.ds(pl.multiple_of(k * (8 * STEP) + (i + j) * 8, 8), 8)) for j in range(4)]
                for a, b in ((0, 1), (2, 3), (0, 2), (1, 3), (1, 2)):
                    order(v, a, b)
                best = merge_best(best, v)
            return tuple(best)

        low = jnp.full((8, 128), -jnp.inf, jnp.float32)
        best = lax.fori_loop(0, 128 // STEP, step, (low, low, low, low))
        for shift in (6, 7):
            best = merge_best(best, [pltpu.roll(b, shift, 0) for b in best])
        scale = wc[r, 9:10, :]
        for j in range(TOP):
            o_ref[0, j, pl.ds(r, 1), :] = best[j][0:1] * scale
            o_ref[1, j, pl.ds(r, 1), :] = best[j][4:5] * scale
        return carry

    lax.fori_loop(0, ROWS_DEV, scan_row, 0)


def send(src, dst, sems, i, device):
    return pltpu.make_async_remote_copy(
        src_ref=src,
        dst_ref=dst,
        send_sem=sems.at[0, i],
        recv_sem=sems.at[1, i],
        device_id=device,
        device_id_type=pl.DeviceIdType.MESH,
    )


COPIES = 64
BATCH = 3


def index_kernel(x_hbm, k1_ref, k2_ref, eye_ref, order_ref, m_ref, nm_ref, dict_ref, o_ref,
                 xbuf, xs, h, c, d, own, sib, st, eout, ein, cout, cin,
                 et, p, f8, u, w, wc, we, inv, xsem, sems):
    strip, slot = lax.axis_index("strip"), lax.axis_index("dict")
    core, zl = slot % 2, slot // 2
    zh, ix, iy = strip // 16, (strip // 4) % 4, strip % 4
    iz = zh * 2 + zl

    def chip(x, y, z):
        x, y, z = x % 4, y % 4, z % 4
        return ((z // 2) * 16 + x * 4 + y, (z % 2) * 2 + core)

    sibling = (strip, zl * 2 + (1 - core))
    x_up, x_down = chip(ix + 1, iy, iz), chip(ix + 3, iy, iz)
    y_up, y_down = chip(ix, iy + 1, iz), chip(ix, iy + 3, iz)
    z_up, z_down = chip(ix, iy, iz + 1), chip(ix, iy, iz + 3)
    row_up, row_down = ((strip + 31) % 32, slot), ((strip + 1) % 32, slot)
    col_left, col_right = (strip, (slot + 3) % 4), (strip, (slot + 1) % 4)

    def fetch(g, at):
        rows = pl.ds(pl.multiple_of(g * (BATCH * RUN), BATCH * RUN), BATCH * RUN)
        return pltpu.make_async_copy(x_hbm.at[rows], xbuf.at[at], xsem.at[at])

    fetch(0, 0).start()
    peers = (sibling, x_up, x_down, y_up, y_down, z_up, z_down, row_up, row_down, col_left, col_right)
    barrier = pltpu.get_barrier_semaphore()
    for peer in peers:
        pl.semaphore_signal(barrier, inc=1, device_id=peer, device_id_type=pl.DeviceIdType.MESH)
    prepare(dict_ref, order_ref, own)
    exchange = send(own, sib, sems, 0, sibling)

    base = pl.multiple_of(core * 1920, 128)
    half = pl.ds(base, 1920)
    mine = {"x": ix, "y": iy, "z": iz}
    ring = {"x": (x_up, x_down), "y": (y_up, y_down), "z": (z_up, z_down)}
    count = iter(range(1, 64))

    def region(lanes, **at):
        where = {axis: at.get(axis, pl.ds(0, 4)) for axis in "xyz"}
        return d.at[where["x"], where["z"], where["y"], :, lanes]

    def same(ref, device):
        return send(ref, ref, sems, next(count), device)

    firsts, seconds = ([], [], []), ([], [], [])
    shared = ([], [], [])
    for part, order_of in enumerate(("yzx", "zxy", "xyz")):
        begin_at = base + 640 * part
        lanes = pl.ds(pl.multiple_of(begin_at, 128), 640)
        ahead = pl.ds(pl.multiple_of(begin_at, 128), 384)
        behind = pl.ds(pl.multiple_of(begin_at + 384, 128), 256)
        for phase, axis in enumerate(order_of):
            at = {other: mine[other] for other in order_of[phase + 1 :]}
            up, down = ring[axis]
            here, after, before = mine[axis], (mine[axis] + 1) % 4, (mine[axis] + 3) % 4
            block = region(lanes, **at, **{axis: here})
            firsts[phase].extend((same(block, up), same(block, down)))
            seconds[phase].append(same(region(ahead, **at, **{axis: before}), up))
            seconds[phase].append(same(region(behind, **at, **{axis: after}), down))
            if phase == 2:
                shared[0].append(same(block, sibling))
                shared[1].append(same(region(lanes, **{axis: before}), sibling))
                shared[1].append(same(region(lanes, **{axis: after}), sibling))
                shared[2].append(same(region(lanes, **{axis: (here + 2) % 4}), sibling))
    stages = (
        firsts[0], seconds[0], firsts[1], seconds[1],
        firsts[2] + shared[0], seconds[2] + shared[1], shared[2],
    )

    def start(copies):
        for copy in copies:
            copy.start()

    def arrive(copies):
        for copy in copies:
            copy.wait_recv()

    def begin():
        exchange.wait_recv()
        ours, theirs = own[:, half], sib[:, half]
        first = core == 0
        both = jnp.concatenate([jnp.where(first, ours, theirs), jnp.where(first, theirs, ours)], axis=0)
        d[ix, iz, iy, :, half] = both.astype(jnp.bfloat16)
        start(stages[0])

    def forward(stage):
        arrive(stages[stage - 1])
        start(stages[stage])

    st[pl.ds(0, LEAD), :] = jnp.zeros((LEAD, DEPTH), jnp.bfloat16)
    tail = LANES - 10 * PITCH
    st[pl.ds(LEAD + 10 * PITCH, tail), :] = jnp.zeros((tail, DEPTH), jnp.bfloat16)
    w[...] = jnp.zeros_like(w)
    f8[...] = jnp.zeros_like(f8)
    usable_rows(nm_ref, u, strip * ROWS_DEV, slot * COLS_DEV, 32 * ROWS_DEV, 4 * COLS_DEV)

    def chunk(g, carry):
        at = g % 2

        @pl.when(g + 1 < GROUPS // BATCH)
        def _():
            fetch(g + 1, 1 - at).start()

        fetch(g, at).wait()
        for i in range(BATCH):
            first_pass(g * BATCH + i, xbuf.at[at, pl.ds(i * RUN, RUN)], k1_ref, xs.at[i], h, c)
        return carry

    lax.fori_loop(0, GROUPS // BATCH, chunk, 0)

    row_copies = [
        send(st.at[pl.ds(own_start(7), 128), :], st.at[pl.ds(own_start(-1), 128), :], sems, 56, row_down),
        send(st.at[pl.ds(own_start(0), 128), :], st.at[pl.ds(own_start(8), 128), :], sems, 57, row_up),
    ]
    edge_copies = [
        send(eout.at[0], ein.at[1], sems, 58, col_left),
        send(eout.at[1], ein.at[0], sems, 59, col_right),
    ]
    corner_copies = [
        send(cout.at[0], cin.at[1], sems, 60, row_up),
        send(cout.at[1], cin.at[0], sems, 61, row_down),
    ]
    pl.semaphore_wait(barrier, len(peers))
    exchange.start()
    second_pass(3, k2_ref, eye_ref, m_ref, h, c, st)
    row_copies[0].start()
    begin()
    second_pass(0, k2_ref, eye_ref, m_ref, h, c, st)
    row_copies[1].start()
    second_pass(1, k2_ref, eye_ref, m_ref, h, c, st)
    forward(1)
    second_pass(2, k2_ref, eye_ref, m_ref, h, c, st)
    own_edges(st, et, eout)
    start(edge_copies)
    forward(2)
    arrive(edge_copies)
    inner_edges(ein, st, et, cout)
    start(corner_copies)
    forward(3)
    gram_fields(st, f8, 2, 4, lambda i: i)
    forward(4)
    gram_fields(st, f8, 4, 5, lambda i: i)
    arrive(corner_copies)
    corner_edges(cin, st, et)
    arrive(row_copies)
    gram_fields(st, f8, 0, 4, lambda i: i + 3 * (i // 2))
    forward(5)
    weigh(f8, u, w)
    spread(w, wc, we)
    forward(6)
    arrive(stages[6])
    entry_norms(d, inv)
    own_products(d, st, p)
    edge_products(d, st, et, p)
    edge_mix(p, we)
    best_scores(p, inv, wc, o_ref)
    everything = [exchange] + row_copies + edge_copies + corner_copies
    for stage in stages:
        everything += stage
    for copy in everything:
        copy.wait_send()


def on_device(patterns, scan_mask, neighbour_mask, dictionary):
    k1, k2, eye, order_t = tables()
    vmem = pl.BlockSpec(memory_space=pltpu.VMEM)
    bf, f32 = jnp.bfloat16, jnp.float32
    return pl.pallas_call(
        index_kernel,
        in_specs=[pl.BlockSpec(memory_space=pl.ANY)] + [vmem] * 7,
        out_specs=vmem,
        out_shape=jax.ShapeDtypeStruct((2, TOP, ROWS_DEV, COLS_DEV), f32),
        scratch_shapes=[
            pltpu.VMEM((2, BATCH * RUN, ROWS_DEV, COLS_DEV), bf),
            pltpu.VMEM((BATCH, RUN * 8, 128), f32),
            pltpu.VMEM((4, GROUPS, RUN, 256), bf),
            pltpu.VMEM((4, GROUPS, GROUPS, 16, 256), f32),
            pltpu.VMEM((4, 4, 4, 16, DEPTH), bf),
            pltpu.VMEM((8, DEPTH), f32),
            pltpu.VMEM((8, DEPTH), f32),
            pltpu.VMEM((HELD, DEPTH), bf),
            pltpu.VMEM((2, 16, DEPTH), bf),
            pltpu.VMEM((2, 16, DEPTH), bf),
            pltpu.VMEM((2, 16, DEPTH), bf),
            pltpu.VMEM((2, 16, DEPTH), bf),
            pltpu.VMEM((32, DEPTH), f32),
            pltpu.VMEM((11, 1024, 128), f32),
            pltpu.VMEM((9, 8, LANES), f32),
            pltpu.VMEM((8, LANES), f32),
            pltpu.VMEM((16, LANES), f32),
            pltpu.VMEM((8, 16, 128), f32),
            pltpu.VMEM((8, 128), f32),
            pltpu.VMEM((1024, 128), f32),
            pltpu.SemaphoreType.DMA((2,)),
            pltpu.SemaphoreType.DMA((2, COPIES)),
        ],
        compiler_params=pltpu.CompilerParams(
            vmem_limit_bytes=67_043_328, collective_id=0, has_side_effects=True
        ),
        name="index",
    )(patterns, k1, k2, eye, order_t, scan_mask, neighbour_mask, dictionary)


def solution(mesh):
    in_specs = (
        P(None, "strip", "dict"),
        P("strip", "dict"),
        P(None, "strip", "dict"),
        P(None, ("strip", "dict"), None),
    )
    out_specs = P(None, None, "strip", "dict")
    return jax.shard_map(
        on_device, mesh=mesh, in_specs=in_specs, out_specs=out_specs, check_vma=False
    )
```

```python
import functools

import jax
import jax.numpy as jnp
import numpy as np
from jax import lax
from jax.experimental import pallas as pl
from jax.experimental.pallas import tpu as pltpu
from jax.sharding import PartitionSpec as P

PH = 60
NPIX = PH * PH
TOP = 4
epsilon = 1e-05
nlpar_scale = 2.0

GROUPS = 15
RUN = 240
RUN_PAD = 256
DEPTH = GROUPS * RUN_PAD
PITCH = 160
LEAD = 336
COLS_DEV = 128
ROWS_DEV = 8
TILES = 7
LANES = TILES * 256
HELD = LEAD + LANES
OFFSETS = tuple(PITCH * a + b for a in (-1, 0, 1) for b in (-1, 0, 1))
NT = (((1,), (1,)), ((), ()))


def tables():
    positions = np.arange(PH, dtype=np.float64)
    spread_px = PH / 8.0
    profile = np.exp(-((positions[:, None] - positions[None, :]) ** 2) / (2.0 * spread_px**2))
    k = profile / profile.sum(axis=1, keepdims=True)
    q = np.arange(RUN)
    d, low = (q // 16) * 4 + (q // 4) % 4, q % 4
    src_a, src_b = q // PH, q % PH
    same = low[:, None] == src_a[None, :]
    first = np.where(same, k[d[:, None], src_b[None, :]], 0.0)
    order = np.where(same & (d[:, None] == src_b[None, :]), 1.0, 0.0)
    e = (q // 16) * 4 + low
    d4 = (q // 4) % 4
    second = np.where(d4[:, None] == d4[None, :], k[e[:, None], e[None, :]], 0.0)
    bf = functools.partial(jnp.asarray, dtype=jnp.bfloat16)
    order_t = np.zeros((RUN, RUN_PAD))
    order_t[:, :RUN] = order.T
    return bf(np.concatenate([first, order])), bf(second), bf(np.eye(256)), bf(order_t)


def prepare(d_ref, order_ref, own):
    x = jnp.concatenate([d_ref[0].astype(jnp.float32), d_ref[1].astype(jnp.float32)], axis=0)
    inv = 1.0 / jnp.sqrt(jnp.sum(x * x, axis=1, keepdims=True) / NPIX + epsilon)
    hi = inv.astype(jnp.bfloat16).astype(jnp.float32)
    mid = (inv - hi).astype(jnp.bfloat16).astype(jnp.float32)
    low = inv - hi - mid
    xb = x.astype(jnp.bfloat16)
    for ge in range(GROUPS):
        run = xb[:, ge * RUN : (ge + 1) * RUN]
        out = jnp.dot(run, order_ref[...], preferred_element_type=jnp.float32)
        if ge == GROUPS - 1:
            lane = lax.broadcasted_iota(jnp.int32, out.shape, 1)
            for i, piece in enumerate((hi, mid, low)):
                out = jnp.where(lane == RUN + i, piece, out)
        own[:, ge * RUN_PAD : (ge + 1) * RUN_PAD] = out


def first_pass(g, x_ref, k1_ref, xs, h, c):
    for j in range(6):
        part = x_ref[pl.ds(j * 40, 40)].astype(jnp.float32)
        xs[pl.ds(j * 320, 320), :] = part.reshape(320, 128)
    h_at = pl.ds(pl.multiple_of(g * 16, 16), 16)
    for n in range(4):
        even = xs[pl.ds(2 * n, RUN, stride=8), :].astype(jnp.bfloat16)
        odd = xs[pl.ds(2 * n + 1, RUN, stride=8), :].astype(jnp.bfloat16)
        pair = jnp.concatenate([even, odd], axis=1)
        out = jnp.dot(k1_ref[...], pair, preferred_element_type=jnp.float32)
        h[n, :, h_at, :] = out[:RUN].astype(jnp.bfloat16).reshape(GROUPS, 16, 256)
        c[n, g] = out[RUN:].reshape(GROUPS, 16, 256)


def second_pass(n, k2_ref, eye_ref, m_ref, h, c, st):
    def second(dc, carry):
        total, square = carry
        out = jnp.dot(k2_ref[...], h[n, dc], preferred_element_type=jnp.float32)
        corrected = c[n, :, dc] - out.reshape(GROUPS, 16, 256)
        c[n, :, dc] = corrected
        part = corrected.reshape(2 * GROUPS, 8, 256)
        return total + jnp.sum(part, axis=0), square + jnp.sum(part * part, axis=0)

    zero = jnp.zeros((8, 256), jnp.float32)
    total, square = lax.fori_loop(0, GROUPS, second, (zero, zero), unroll=15)
    mean = jnp.sum(total, axis=0, keepdims=True) / NPIX
    var = jnp.sum(square, axis=0, keepdims=True) / NPIX - mean * mean
    mask = jnp.concatenate([m_ref[2 * n : 2 * n + 1, :], m_ref[2 * n + 1 : 2 * n + 2, :]], axis=1)
    scale = mask.astype(jnp.float32) / jnp.sqrt(jnp.maximum(var, 0.0) + epsilon)
    shift = mean * scale

    def third(ge, carry):
        v = (c[n, ge].reshape(RUN, 256) * scale - shift).astype(jnp.bfloat16)
        v = jnp.concatenate([v, jnp.zeros((16, 256), jnp.bfloat16)], axis=0)
        out = lax.dot_general(eye_ref[...], v, NT, preferred_element_type=jnp.float32)
        out = out.astype(jnp.bfloat16)
        at = pl.ds(pl.multiple_of(ge * RUN_PAD, RUN_PAD), RUN_PAD)
        st[pl.ds(own_start(2 * n), 128), at] = out[:128]
        st[pl.ds(own_start(2 * n + 1), 128), at] = out[128:]
        return carry

    lax.fori_loop(0, GROUPS, third, 0, unroll=15)


def row_start(scan_row):
    return LEAD + PITCH * scan_row


def own_start(r):
    return row_start(r + 1) + 16


def gram_fields(st, f8, begin, end, tile_of):
    row_at = lax.broadcasted_iota(jnp.int32, (136, 128), 0)
    lane_at = lax.broadcasted_iota(jnp.int32, (136, 128), 1)
    slots = {}
    for kk in range(9):
        for low in range(min(kk + 1, 8)):
            slots.setdefault(OFFSETS[kk] - OFFSETS[low], []).append((kk, low))

    def tile(i, carry):
        n0 = pl.multiple_of(tile_of(i) * 256, 256)
        rows = st[pl.ds(n0, LEAD + 256), :]
        cols = st[pl.ds(pl.multiple_of(n0 + LEAD, 16), 256), :]
        g = lax.dot_general(rows, cols, NT, preferred_element_type=jnp.float32)
        for half in range(2):
            lanes = g[:, half * 128 : (half + 1) * 128]
            for o, where_to in slots.items():
                first = LEAD + half * 128 - o
                start = min(first // 8 * 8, LEAD + 256 - 136)
                hit = row_at + (start - first) == lane_at
                value = jnp.sum(jnp.where(hit, lanes[start : start + 136], 0.0), axis=0, keepdims=True)
                at = pl.ds(pl.multiple_of(n0 + half * 128, 128), 128)
                for kk, low in where_to:
                    f8[kk, low : low + 1, at] = value
        return carry

    lax.fori_loop(begin, end, tile, 0)


def usable_rows(nm_ref, u, first_row, first_col, all_rows, all_cols):
    u[...] = jnp.zeros_like(u)
    kk = lax.broadcasted_iota(jnp.int32, (8, 128), 0)
    kk = kk + (kk >= 4).astype(jnp.int32)
    down = (kk >= 3).astype(jnp.int32) + (kk >= 6).astype(jnp.int32) - 1
    right = kk - 3 * (down + 1) - 1
    col = lax.broadcasted_iota(jnp.int32, (8, 128), 1) + first_col + right
    col_ok = (col >= 0) & (col < all_cols)
    for r in range(ROWS_DEV):
        row = down + (first_row + r)
        ok = (row >= 0) & (row < all_rows) & col_ok & (nm_ref[:, r, :] == 1)
        at = PITCH * (r + 1) + 16
        u[:, at : at + 128] = ok.astype(jnp.float32)


def weigh(f8, u, w):
    def turn(x, off):
        return x if off == 0 else pltpu.roll(x, (-off) % LANES, 1)

    n = f8[0, 0:1, :]
    centre = f8[4]
    placed = {4: centre}
    for kk in (0, 1, 2, 3, 5, 6, 7, 8):
        placed[kk] = turn(f8[kk], OFFSETS[kk])
    last = turn(jnp.broadcast_to(n, (8, LANES)), OFFSETS[8])[0:1]
    own = [placed[kk][kk : kk + 1] if kk < 8 else last for kk in range(9)]
    den = jnp.ones((1, LANES), jnp.float32)
    weights = []
    for kk in range(9):
        if kk == 4:
            value = jnp.ones((1, LANES), jnp.float32)
        else:
            dot = centre[kk : kk + 1] if kk < 4 else placed[kk][4:5]
            distance = (n + own[kk] - 2.0 * dot) / NPIX
            slot = kk if kk < 4 else kk - 1
            value = jnp.where(u[slot : slot + 1, :] > 0.5, jnp.exp(-distance / nlpar_scale), 0.0)
            den = den + value
        weights.append(value)
        w[kk : kk + 1, :] = value
    lows = w[0:8, :]
    quad = jnp.zeros((1, LANES), jnp.float32)
    for kk in range(9):
        part = 2.0 * jnp.sum(lows * placed[kk], axis=0, keepdims=True)
        self_term = weights[kk] * own[kk]
        part = part - self_term if kk < 8 else part + self_term
        quad = quad + weights[kk] * part
    square = jnp.maximum(quad, 0.0) / (den * den) / NPIX
    w[9:10, :] = 1.0 / (jnp.sqrt(square + epsilon) * den * NPIX)


def spread(w, wc, we):
    lane = lax.broadcasted_iota(jnp.int32, (16, 128), 1)
    edge = jnp.zeros((16, 128), jnp.float32)
    kinds = lax.broadcasted_iota(jnp.int32, (16, 128), 0)
    left = (kinds == 0) | (kinds == 3) | (kinds == 6)
    right = (kinds == 2) | (kinds == 5) | (kinds == 8)
    for r in range(ROWS_DEV):
        at = PITCH * (r + 1) + 16
        here = w[:, at : at + 128]
        before = w[:, at + 1 : at + 129]
        after = w[:, at - 1 : at + 127]
        wc[r] = jnp.where(left, before, jnp.where(right, after, here))
        R = r + 1
        edge = jnp.where(lane == 2 * R, pltpu.roll(here, 2 * R, 1), edge)
        edge = jnp.where(lane == 2 * R + 1, pltpu.roll(here, 2 * R + 2, 1), edge)
    odd = lane[0:1] % 2 == 1
    for i in range(3):
        we[i : i + 1, :] = jnp.where(odd, edge[3 * i + 2 : 3 * i + 3], edge[3 * i : 3 * i + 1])


def own_edges(st, et, eout):
    for r in range(ROWS_DEV):
        top = own_start(r)
        et[r : r + 1, :] = st[pl.ds(top, 16), :].astype(jnp.float32)[0:1]
        et[16 + r : 17 + r, :] = st[pl.ds(top + 112, 16), :].astype(jnp.float32)[15:16]
    et[8:16, :] = jnp.zeros((8, DEPTH), jnp.float32)
    et[24:32, :] = jnp.zeros((8, DEPTH), jnp.float32)
    eout[0] = et[0:16, :].astype(jnp.bfloat16)
    eout[1] = et[16:32, :].astype(jnp.bfloat16)


def place_edges(R, left, right, st, et):
    et[2 * R : 2 * R + 1, :] = left
    et[2 * R + 1 : 2 * R + 2, :] = right
    st[pl.ds(row_start(R), 16), :] = jnp.broadcast_to(left, (16, DEPTH)).astype(jnp.bfloat16)
    st[pl.ds(row_start(R) + 144, 16), :] = jnp.broadcast_to(right, (16, DEPTH)).astype(jnp.bfloat16)


def inner_edges(ein, st, et, cout):
    left, right = ein[0].astype(jnp.float32), ein[1].astype(jnp.float32)
    row = lax.broadcasted_iota(jnp.int32, (16, DEPTH), 0)
    for i, r in enumerate((0, ROWS_DEV - 1)):
        both = jnp.where(row == 0, left[r : r + 1], right[r : r + 1])
        cout[i] = both.astype(jnp.bfloat16)
    for r in range(ROWS_DEV):
        place_edges(r + 1, left[r : r + 1], right[r : r + 1], st, et)


def corner_edges(cin, st, et):
    for i, R in enumerate((0, ROWS_DEV + 1)):
        both = cin[i].astype(jnp.float32)
        place_edges(R, both[0:1], both[1:2], st, et)
    et[20:32, :] = jnp.zeros((12, DEPTH), jnp.float32)


def pair_product(d, st, p, i, j):
    a = pl.multiple_of(LEAD + 16 + PITCH * i, 16)
    b = pl.multiple_of(LEAD + 16 + PITCH * j, 16)
    rows = jnp.concatenate([st[pl.ds(a, 128), :], st[pl.ds(b, 128), :]], axis=0)
    out = lax.dot_general(d[...].reshape(1024, DEPTH), rows, NT, preferred_element_type=jnp.float32)
    p[i] = out[:, :128]
    p[j] = out[:, 128:]


def own_products(d, st, p):
    def pair(i, carry):
        pair_product(d, st, p, 2 * i + 1, 2 * i + 2)
        return carry

    lax.fori_loop(0, ROWS_DEV // 2, pair, 0)


def edge_products(d, et, p):
    edge = et[...].astype(jnp.bfloat16)
    edge = jnp.concatenate([edge, jnp.zeros((96, DEPTH), jnp.bfloat16)], axis=0)
    p[10] = lax.dot_general(d[...].reshape(1024, DEPTH), edge, NT, preferred_element_type=jnp.float32)


def entry_norms(d, inv):
    tail = d[:, :, :, DEPTH - 128 :].reshape(1024, 128).astype(jnp.float32)
    at = RUN - 128
    value = tail[:, at : at + 1] + tail[:, at + 1 : at + 2] + tail[:, at + 2 : at + 3]
    inv[...] = jnp.broadcast_to(value, inv.shape)


def edge_mix(p, we):
    def step(k, carry):
        at = pl.ds(pl.multiple_of(k * 8, 8), 8)
        e = p[10, at, :]
        mix = e * we[1:2, :] + pltpu.roll(e, 2, 1) * we[0:1, :] + pltpu.roll(e, 126, 1) * we[2:3, :]
        p[10, at, :] = mix
        return carry

    lax.fori_loop(0, 128, step, 0, unroll=16)


def order(x, i, j):
    x[i], x[j] = jnp.maximum(x[i], x[j]), jnp.minimum(x[i], x[j])


def merge_best(best, other):
    m = [jnp.maximum(best[i], other[3 - i]) for i in range(4)]
    for i, j in ((0, 2), (1, 3), (0, 1), (2, 3)):
        order(m, i, j)
    return m


STEP = 32


def best_scores(p, inv, wc, o_ref):
    lane = lax.broadcasted_iota(jnp.int32, (8, 128), 1)
    first, last = lane == 0, lane == 127

    def scan_row(r, carry):
        wt = [jnp.broadcast_to(wc[r, kk : kk + 1, :], (8, 128)) for kk in range(9)]
        turn = 125 - 2 * r

        def score(at):
            up, mid, down = p[r, at, :], p[r + 1, at, :], p[r + 2, at, :]
            edge = pltpu.roll(p[10, at, :], turn, 1)
            left = up * wt[0] + mid * wt[3] + down * wt[6]
            right = up * wt[2] + mid * wt[5] + down * wt[8]
            here = up * wt[1] + mid + down * wt[7]
            left = jnp.where(last, edge, left)
            right = jnp.where(first, edge, right)
            return (here + pltpu.roll(left, 1, 1) + pltpu.roll(right, 127, 1)) * inv[at, :]

        def step(k, best):
            best = list(best)
            for i in range(0, STEP, 4):
                v = [score(pl.ds(pl.multiple_of(k * (8 * STEP) + (i + j) * 8, 8), 8)) for j in range(4)]
                for a, b in ((0, 1), (2, 3), (0, 2), (1, 3), (1, 2)):
                    order(v, a, b)
                best = merge_best(best, v)
            return tuple(best)

        low = jnp.full((8, 128), -jnp.inf, jnp.float32)
        best = lax.fori_loop(0, 128 // STEP, step, (low, low, low, low))
        for shift in (6, 7):
            best = merge_best(best, [pltpu.roll(b, shift, 0) for b in best])
        scale = wc[r, 9:10, :]
        for j in range(TOP):
            o_ref[0, j, pl.ds(r, 1), :] = best[j][0:1] * scale
            o_ref[1, j, pl.ds(r, 1), :] = best[j][4:5] * scale
        return carry

    lax.fori_loop(0, ROWS_DEV, scan_row, 0)


def send(src, dst, sems, i, device):
    return pltpu.make_async_remote_copy(
        src_ref=src,
        dst_ref=dst,
        send_sem=sems.at[0, i],
        recv_sem=sems.at[1, i],
        device_id=device,
        device_id_type=pl.DeviceIdType.MESH,
    )


COPIES = 48
BATCH = 3


def index_kernel(x_hbm, k1_ref, k2_ref, eye_ref, order_ref, m_ref, nm_ref, dict_ref, o_ref,
                 xbuf, xs, h, c, d, own, sib, st, eout, ein, cout, cin,
                 et, p, f8, u, w, wc, we, inv, xsem, sems):
    strip, slot = lax.axis_index("strip"), lax.axis_index("dict")
    core, zl = slot % 2, slot // 2
    zh, ix, iy = strip // 16, (strip // 4) % 4, strip % 4
    iz = zh * 2 + zl

    def chip(x, y, z):
        x, y, z = x % 4, y % 4, z % 4
        return ((z // 2) * 16 + x * 4 + y, (z % 2) * 2 + core)

    sibling = (strip, zl * 2 + (1 - core))
    x_up, x_down = chip(ix + 1, iy, iz), chip(ix + 3, iy, iz)
    y_up, y_down = chip(ix, iy + 1, iz), chip(ix, iy + 3, iz)
    z_up, z_down = chip(ix, iy, iz + 1), chip(ix, iy, iz + 3)
    row_up, row_down = ((strip + 31) % 32, slot), ((strip + 1) % 32, slot)
    col_left, col_right = (strip, (slot + 3) % 4), (strip, (slot + 1) % 4)

    def fetch(g, at):
        rows = pl.ds(pl.multiple_of(g * (BATCH * RUN), BATCH * RUN), BATCH * RUN)
        return pltpu.make_async_copy(x_hbm.at[rows], xbuf.at[at], xsem.at[at])

    fetch(0, 0).start()
    peers = (sibling, x_up, x_down, y_up, y_down, z_up, z_down, row_up, row_down, col_left, col_right)
    barrier = pltpu.get_barrier_semaphore()
    for peer in peers:
        pl.semaphore_signal(barrier, inc=1, device_id=peer, device_id_type=pl.DeviceIdType.MESH)
    prepare(dict_ref, order_ref, own)
    exchange = send(own, sib, sems, 0, sibling)

    base = pl.multiple_of(core * 1920, 128)
    half = pl.ds(base, 1920)
    part_a = pl.ds(base, 1024)
    part_b = pl.ds(pl.multiple_of(base + 1024, 128), 896)
    xu, xd, yu, yd, zu, zd = [(v % 4) for v in (ix + 1, ix + 3, iy + 1, iy + 3, iz + 1, iz + 3)]

    def same(ref, i, device):
        return send(ref, ref, sems, i, device)

    def rows_of(y):
        return pl.ds(pl.multiple_of(y * 16, 16), 16)

    upper, lower = pl.ds(0, 32), pl.ds(32, 32)
    y_first = [same(d.at[ix, iz, rows_of(iy), half], 1, y_up), same(d.at[ix, iz, rows_of(iy), half], 2, y_down)]
    y_second = [same(d.at[ix, iz, rows_of(yd), part_a], 3, y_up), same(d.at[ix, iz, rows_of(yu), part_b], 4, y_down)]
    mid_first = [
        same(d.at[ix, iz, :, part_a], 5, z_up),
        same(d.at[ix, iz, :, part_a], 6, z_down),
        same(d.at[ix, iz, :, part_b], 7, x_up),
        same(d.at[ix, iz, :, part_b], 8, x_down),
    ]
    mid_second = [
        same(d.at[ix, zd, upper, part_a], 9, z_up),
        same(d.at[ix, zu, lower, part_a], 10, z_down),
        same(d.at[xd, iz, upper, part_b], 11, x_up),
        same(d.at[xu, iz, lower, part_b], 12, x_down),
    ]
    last_first = [
        same(d.at[ix, :, :, part_a], 13, x_up),
        same(d.at[ix, :, :, part_a], 14, x_down),
        same(d.at[:, iz, :, part_b], 15, z_up),
        same(d.at[:, iz, :, part_b], 16, z_down),
        same(d.at[ix, :, :, part_a], 17, sibling),
        same(d.at[:, iz, :, part_b], 18, sibling),
    ]
    first_two, last_two = pl.ds(0, 2), pl.ds(2, 2)
    last_second = [
        same(d.at[xd, first_two, :, part_a], 19, x_up),
        same(d.at[xu, last_two, :, part_a], 20, x_down),
        same(d.at[first_two, zd, :, part_b], 21, z_up),
        same(d.at[last_two, zu, :, part_b], 22, z_down),
        same(d.at[xd, :, :, part_a], 23, sibling),
        same(d.at[xu, :, :, part_a], 24, sibling),
        same(d.at[:, zd, :, part_b], 25, sibling),
        same(d.at[:, zu, :, part_b], 26, sibling),
    ]
    xo, zo = (ix + 2) % 4, (iz + 2) % 4
    final = [
        same(d.at[xo, :, :, part_a], 27, sibling),
        same(d.at[:, zo, :, part_b], 28, sibling),
    ]

    def start(copies):
        for copy in copies:
            copy.start()

    def arrive(copies):
        for copy in copies:
            copy.wait_recv()

    def begin():
        exchange.wait_recv()
        mine, other = own[:, half], sib[:, half]
        first = core == 0
        both = jnp.concatenate([jnp.where(first, mine, other), jnp.where(first, other, mine)], axis=0)
        d[ix, iz, rows_of(iy), half] = both.astype(jnp.bfloat16)
        start(y_first)

    def forward(arrived, following):
        def act():
            arrive(arrived)
            start(following)
        return act

    st[pl.ds(0, LEAD), :] = jnp.zeros((LEAD, DEPTH), jnp.bfloat16)
    tail = LANES - 10 * PITCH
    st[pl.ds(LEAD + 10 * PITCH, tail), :] = jnp.zeros((tail, DEPTH), jnp.bfloat16)
    w[...] = jnp.zeros_like(w)
    f8[...] = jnp.zeros_like(f8)
    usable_rows(nm_ref, u, strip * ROWS_DEV, slot * COLS_DEV, 32 * ROWS_DEV, 4 * COLS_DEV)

    def chunk(g, carry):
        at = g % 2

        @pl.when(g + 1 < GROUPS // BATCH)
        def _():
            fetch(g + 1, 1 - at).start()

        fetch(g, at).wait()
        for i in range(BATCH):
            first_pass(g * BATCH + i, xbuf.at[at, pl.ds(i * RUN, RUN)], k1_ref, xs.at[i], h, c)
        return carry

    lax.fori_loop(0, GROUPS // BATCH, chunk, 0)

    row_copies = [
        send(st.at[pl.ds(own_start(7), 128), :], st.at[pl.ds(own_start(-1), 128), :], sems, 29, row_down),
        send(st.at[pl.ds(own_start(0), 128), :], st.at[pl.ds(own_start(8), 128), :], sems, 30, row_up),
    ]
    edge_copies = [
        send(eout.at[0], ein.at[1], sems, 31, col_left),
        send(eout.at[1], ein.at[0], sems, 32, col_right),
    ]
    corner_copies = [
        send(cout.at[0], cin.at[1], sems, 33, row_up),
        send(cout.at[1], cin.at[0], sems, 34, row_down),
    ]
    def start_rows(turning):
        pl.when((iy == 3) == turning)(row_copies[0].start)
        pl.when((iy == 0) == turning)(row_copies[1].start)

    pl.semaphore_wait(barrier, len(peers))
    exchange.start()
    second_pass(3, k2_ref, eye_ref, m_ref, h, c, st)
    begin()
    second_pass(0, k2_ref, eye_ref, m_ref, h, c, st)
    second_pass(1, k2_ref, eye_ref, m_ref, h, c, st)
    forward(y_first, y_second)()
    start_rows(False)
    second_pass(2, k2_ref, eye_ref, m_ref, h, c, st)
    own_edges(st, et, eout)
    start(edge_copies)
    forward(y_second, mid_first)()
    arrive(edge_copies)
    inner_edges(ein, st, et, cout)
    start(corner_copies)
    forward(mid_first, mid_second)()
    gram_fields(st, f8, 2, 4, lambda i: i)
    forward(mid_second, last_first)()
    gram_fields(st, f8, 4, 5, lambda i: i)
    forward(last_first, last_second)()
    start_rows(True)
    arrive(corner_copies)
    corner_edges(cin, st, et)
    forward(last_second, final)()
    arrive(final)
    entry_norms(d, inv)
    own_products(d, st, p)
    edge_products(d, et, p)
    arrive(row_copies)
    pair_product(d, st, p, 0, ROWS_DEV + 1)
    gram_fields(st, f8, 0, 4, lambda i: i + 3 * (i // 2))
    weigh(f8, u, w)
    spread(w, wc, we)
    edge_mix(p, we)
    best_scores(p, inv, wc, o_ref)
    everything = [exchange] + y_first + y_second + mid_first + mid_second + last_first + last_second + final
    for copy in everything + row_copies + edge_copies + corner_copies:
        copy.wait_send()


def on_device(patterns, scan_mask, neighbour_mask, dictionary):
    k1, k2, eye, order_t = tables()
    vmem = pl.BlockSpec(memory_space=pltpu.VMEM)
    bf, f32 = jnp.bfloat16, jnp.float32
    return pl.pallas_call(
        index_kernel,
        in_specs=[pl.BlockSpec(memory_space=pl.ANY)] + [vmem] * 7,
        out_specs=vmem,
        out_shape=jax.ShapeDtypeStruct((2, TOP, ROWS_DEV, COLS_DEV), f32),
        scratch_shapes=[
            pltpu.VMEM((2, BATCH * RUN, ROWS_DEV, COLS_DEV), bf),
            pltpu.VMEM((BATCH, RUN * 8, 128), f32),
            pltpu.VMEM((4, GROUPS, RUN, 256), bf),
            pltpu.VMEM((4, GROUPS, GROUPS, 16, 256), f32),
            pltpu.VMEM((4, 4, 64, DEPTH), bf),
            pltpu.VMEM((8, DEPTH), f32),
            pltpu.VMEM((8, DEPTH), f32),
            pltpu.VMEM((HELD, DEPTH), bf),
            pltpu.VMEM((2, 16, DEPTH), bf),
            pltpu.VMEM((2, 16, DEPTH), bf),
            pltpu.VMEM((2, 16, DEPTH), bf),
            pltpu.VMEM((2, 16, DEPTH), bf),
            pltpu.VMEM((32, DEPTH), f32),
            pltpu.VMEM((11, 1024, 128), f32),
            pltpu.VMEM((9, 8, LANES), f32),
            pltpu.VMEM((8, LANES), f32),
            pltpu.VMEM((16, LANES), f32),
            pltpu.VMEM((8, 16, 128), f32),
            pltpu.VMEM((8, 128), f32),
            pltpu.VMEM((1024, 128), f32),
            pltpu.SemaphoreType.DMA((2,)),
            pltpu.SemaphoreType.DMA((2, COPIES)),
        ],
        compiler_params=pltpu.CompilerParams(
            vmem_limit_bytes=67_043_328, collective_id=0, has_side_effects=True
        ),
        name="index",
    )(patterns, k1, k2, eye, order_t, scan_mask, neighbour_mask, dictionary)


def solution(mesh):
    in_specs = (
        P(None, "strip", "dict"),
        P("strip", "dict"),
        P(None, "strip", "dict"),
        P(None, ("strip", "dict"), None),
    )
    out_specs = P(None, None, "strip", "dict")
    return jax.shard_map(
        on_device, mesh=mesh, in_specs=in_specs, out_specs=out_specs, check_vma=False
    )
```
